512 devices in a mesh: req: 64 (over y, z), tensor: 8 (over x, core).
Axes of the slice: x: 4, y: 4, z: 16, core: 2. Of those that a mesh axis runs over, the one named last changes fastest.
Arguments:
- pre_tokens: bfloat16 [16384, 1024], P('req', 'tensor'), may hold values from -24 to 24
- dec_tokens: bfloat16 [64, 1024], P('req', 'tensor'), may hold values from -24 to 24
- req_of: int32 [64], replicated, may hold values from 0 to 63, each once
- page_table: int32 [64, 16], replicated, may hold values from -1 to 575, as said below
- page_place: int32 [576], replicated, may hold values from 0 to 575, as said below
- cache_lengths: int32 [64], replicated, may hold values from 1 to 2048, as said below
- cache_keys: bfloat16 [576, 128, 1024], P('req', None, 'tensor'), may hold values from -24 to 24
- cache_values: bfloat16 [576, 128, 1024], P('req', None, 'tensor'), may hold values from -6 to 6
- w_qkv: bfloat16 [1024, 3, 1024], P(None, None, 'tensor'), may hold values from -0.1875 to 0.1875
- w_out: bfloat16 [1024, 1024], P('tensor'), may hold values from -0.1875 to 0.1875
- ln1_gain: float32 [1024], replicated, may hold values from 0.5 to 1.5
- ln1_bias: float32 [1024], replicated, may hold values from -1 to 1
- w_up: bfloat16 [1024, 4096], P(None, 'tensor'), may hold values from -0.1875 to 0.1875
- w_down: bfloat16 [4096, 1024], P('tensor'), may hold values from -0.09375 to 0.09375
- ln2_gain: float32 [1024], replicated, may hold values from 0.5 to 1.5
- ln2_bias: float32 [1024], replicated, may hold values from -1 to 1
Outputs:
- pre_out: bfloat16 [16384, 1024], P('req', 'tensor')
- dec_out: bfloat16 [64, 1024], P('req', 'tensor')
The draws below stay inside these ranges and needn't reach their ends.
Inputs may be any that keep to these rules, and one draw needn't show every extreme that they name: `page_table`: entry j of row r is a page id for j < ceil(cache_lengths[r] / 128) and -1 after; no page id appears twice; the requests hold 544 pages together. `page_place`: a permutation; page p sits on index page_place[p] // 9 of req; one index of req holds at most 1 pages of one request, and some holds exactly 1. `cache_lengths`: some request has exactly 2048 tokens.
All inputs are finite; a program needn't handle non-finite values.
Results may differ from the reference program's by a relative error of at most 0.023.
Values may be sent and summed in bfloat16 or wider, within the bound.
A program may use at most 64 MiB of HBM per device.

```python
import math
import jax
import jax.numpy as jnp
from jax import lax

D = 1024
HEADS = 16
HD = 64
FF = 4096
PAGE = 128
MAXP = 16
PRE_LEN = 256
NDEC = 64
PAGES_DEV = 9
PAGES = 576
PRE_ROWS = 16384
N_TENSOR = 8


def token_values(key, count):
    base = jnp.clip(jax.random.normal(key, (count, D), jnp.float32), -4.0, 4.0)
    return base.astype(jnp.bfloat16)


def draw_pre_tokens(key, part):
    return token_values(key, PRE_ROWS)


def draw_dec_tokens(key, part):
    return token_values(jax.random.fold_in(key, 7), NDEC)


def draw_cache_keys(key, part):
    base = 2.0 * jnp.clip(jax.random.normal(key, (PAGES, PAGE, D), jnp.float32), -4.0, 4.0)
    return base.astype(jnp.bfloat16)


def page_layout(key):
    pair_order = jax.random.permutation(jax.random.fold_in(key, 101), NDEC).astype(jnp.int32)
    firsts = jax.random.randint(jax.random.fold_in(key, 102), (NDEC // 2,), 1, MAXP + 1).astype(jnp.int32)
    firsts = firsts.at[0].set(MAXP)
    counts = jnp.zeros((NDEC,), jnp.int32).at[pair_order[0::2]].set(firsts).at[pair_order[1::2]].set(MAXP + 1 - firsts)
    alloc_order = jax.random.permutation(jax.random.fold_in(key, 103), NDEC).astype(jnp.int32)
    ordered = counts[alloc_order]
    begin_ordered = jnp.cumsum(ordered) - ordered
    begin = jnp.zeros((NDEC,), jnp.int32).at[alloc_order].set(begin_ordered.astype(jnp.int32))
    labels = jax.random.permutation(jax.random.fold_in(key, 104), PAGES).astype(jnp.int32)
    steps = jnp.arange(MAXP, dtype=jnp.int32)
    positions = begin[:, None] + steps[None, :]
    valid = steps[None, :] < counts[:, None]
    table = jnp.where(valid, labels[jnp.clip(positions, 0, PAGES - 1)], -1).astype(jnp.int32)
    inverse = jnp.zeros((PAGES,), jnp.int32).at[labels].set(jnp.arange(PAGES, dtype=jnp.int32))
    place = (inverse % NDEC * PAGES_DEV + inverse // NDEC).astype(jnp.int32)
    tails = jax.random.randint(jax.random.fold_in(key, 105), (NDEC,), 1, PAGE + 1).astype(jnp.int32)
    lengths = (counts - 1) * PAGE + tails
    lengths = lengths.at[pair_order[0]].set(MAXP * PAGE).astype(jnp.int32)
    return (table, place, lengths)


def draw_page_table(key, part):
    return page_layout(key)[0]


def draw_page_place(key, part):
    return page_layout(key)[1]


def draw_cache_lengths(key, part):
    return page_layout(key)[2]


def block_levels(stream_key, extent, shards, low, top_value):
    level, own = 1.0, jax.random.fold_in(stream_key, 6)
    for axis_at, parts in shards:
        heights = jnp.exp(jax.random.uniform(jax.random.fold_in(own, axis_at), (parts,), jnp.float32, low / len(shards), top_value / len(shards)))
        level = level * jnp.repeat(heights, extent[axis_at] // parts).reshape([-1 if axis == axis_at else 1 for axis in range(len(extent))])
    return level


def scatter_about(stream_key, extent, scale, limit, split=(), held_as=jnp.bfloat16):
    entries = scale * jax.random.normal(stream_key, extent, jnp.float32)
    if split:
        entries = entries * block_levels(stream_key, extent, split, -0.22, 0.18)
    return jnp.clip(entries, -limit, limit).astype(held_as)


def setup_inputs(seed: int = 0) -> dict:
    streams_of = jax.random.split(jax.random.key(seed), 17)
    pre_tokens = draw_pre_tokens(jax.random.fold_in(streams_of[16], 71), 0)
    dec_tokens = draw_dec_tokens(jax.random.fold_in(streams_of[16], 71), 0)
    req_of = jax.random.permutation(streams_of[2], NDEC).astype(jnp.int32)
    page_table = draw_page_table(jax.random.fold_in(streams_of[16], 71), 0)
    page_place = draw_page_place(jax.random.fold_in(streams_of[16], 71), 0)
    cache_lengths = draw_cache_lengths(jax.random.fold_in(streams_of[16], 71), 0)
    cache_keys = draw_cache_keys(jax.random.fold_in(streams_of[16], 71), 0)
    cache_values = scatter_about(streams_of[7], (PAGES, PAGE, D), 1.0, 6.0, ((0, 64), (2, 8)))
    w_qkv = scatter_about(streams_of[8], (D, 3, D), D ** -0.5, 0.1875, ((2, 8),))
    w_out = scatter_about(streams_of[9], (D, D), D ** -0.5, 0.1875, ((0, 8),))
    ln1_gain = jnp.clip(1.0 + 0.1 * jax.random.normal(streams_of[10], (D,), jnp.float32), 0.5, 1.5)
    ln1_bias = scatter_about(streams_of[11], (D,), 0.2, 1.0, (), jnp.float32)
    w_up = scatter_about(streams_of[12], (D, FF), D ** -0.5, 0.1875, ((1, 8),))
    w_down = scatter_about(streams_of[13], (FF, D), FF ** -0.5, 0.09375, ((0, 8),))
    ln2_gain = jnp.clip(1.0 + 0.1 * jax.random.normal(streams_of[14], (D,), jnp.float32), 0.5, 1.5)
    ln2_bias = scatter_about(streams_of[15], (D,), 0.2, 1.0, (), jnp.float32)
    return dict(pre_tokens=pre_tokens, dec_tokens=dec_tokens, req_of=req_of, page_table=page_table, page_place=page_place, cache_lengths=cache_lengths, cache_keys=cache_keys, cache_values=cache_values, w_qkv=w_qkv, w_out=w_out, ln1_gain=ln1_gain, ln1_bias=ln1_bias, w_up=w_up, w_down=w_down, ln2_gain=ln2_gain, ln2_bias=ln2_bias)


norm_eps = 1e-05
neg_large = -1e+30

def norm_rows(total, gain, shift):
    mean = lax.optimization_barrier(jnp.mean(total, axis=-1, keepdims=True))
    centered = total - mean
    var = lax.optimization_barrier(jnp.mean(centered * centered, axis=-1, keepdims=True))
    return centered * lax.rsqrt(var + norm_eps) * gain + shift

def rounded(values):
    return lax.optimization_barrier(values.astype(jnp.bfloat16)).astype(jnp.float32)

def group_sum(left, right, group_width):
    total = jnp.zeros((left.shape[0], right.shape[1]), jnp.float32)
    for group in range(N_TENSOR):
        low = group * group_width
        term = jnp.dot(left[:, low:low + group_width], right[low:low + group_width], preferred_element_type=jnp.float32)
        total = total + rounded(term)
    return total

def reference(pre_tokens, dec_tokens, req_of, page_table, page_place, cache_lengths, cache_keys, cache_values, w_qkv, w_out, ln1_gain, ln1_bias, w_up, w_down, ln2_gain, ln2_bias):
    scale = 1.0 / math.sqrt(HD)
    flat_qkv = w_qkv.reshape(D, 3 * D)

    def one_slot(inputs):
        pre_rows, dec_row, request = inputs
        rows = jnp.concatenate([pre_rows, dec_row[None]], axis=0)
        mixed = rounded(jnp.dot(rows, flat_qkv, preferred_element_type=jnp.float32))
        mixed = mixed.reshape(PRE_LEN + 1, 3, HEADS, HD)
        query = mixed[:, 0]
        keyed = mixed[:, 1]
        valued = mixed[:, 2]
        scores = jnp.einsum('qhd,khd->hqk', query[:PRE_LEN], keyed[:PRE_LEN]) * scale
        row_pos = jnp.arange(PRE_LEN, dtype=jnp.int32)
        causal = row_pos[:, None] >= row_pos[None, :]
        scores = jnp.where(causal[None], scores, neg_large)
        top = lax.optimization_barrier(jnp.max(scores, axis=-1, keepdims=True))
        weights = jnp.where(causal[None], jnp.exp(scores - top), 0.0)
        total = lax.optimization_barrier(jnp.sum(weights, axis=-1))
        pre_context = jnp.einsum('hqk,khd->qhd', rounded(weights), valued[:PRE_LEN]) / jnp.transpose(total)[:, :, None]
        pre_context = pre_context.astype(jnp.bfloat16).reshape(PRE_LEN, D)
        slots = page_place[jnp.maximum(page_table[request], 0)]
        keys = cache_keys[slots].reshape(MAXP * PAGE, HEADS, HD).astype(jnp.float32)
        values = cache_values[slots].reshape(MAXP * PAGE, HEADS, HD).astype(jnp.float32)
        keys = jnp.concatenate([keys, keyed[PRE_LEN][None]], axis=0)
        values = jnp.concatenate([values, valued[PRE_LEN][None]], axis=0)
        positions = jnp.arange(MAXP * PAGE, dtype=jnp.int32)
        usable = jnp.concatenate([positions < cache_lengths[request], jnp.ones((1,), dtype=bool)])
        dec_scores = jnp.einsum('hd,khd->hk', query[PRE_LEN], keys) * scale
        dec_scores = jnp.where(usable[None], dec_scores, neg_large)
        dec_top = lax.optimization_barrier(jnp.max(dec_scores, axis=-1, keepdims=True))
        dec_weights = jnp.where(usable[None], jnp.exp(dec_scores - dec_top), 0.0)
        dec_total = lax.optimization_barrier(jnp.sum(dec_weights, axis=-1))
        dec_context = jnp.einsum('hk,khd->hd', rounded(dec_weights), values) / dec_total[:, None]
        dec_context = dec_context.astype(jnp.bfloat16).reshape(1, D)
        context = jnp.concatenate([pre_context, dec_context], axis=0)
        attn = group_sum(context, w_out, D // N_TENSOR)
        first = norm_rows(rows.astype(jnp.float32) + attn, ln1_gain, ln1_bias).astype(jnp.bfloat16)
        hidden = jax.nn.gelu(jnp.dot(first, w_up, preferred_element_type=jnp.float32), approximate=False).astype(jnp.bfloat16)
        mlp = group_sum(hidden, w_down, FF // N_TENSOR)
        first_wide = lax.optimization_barrier(first).astype(jnp.float32)
        result = norm_rows(first_wide + mlp, ln2_gain, ln2_bias).astype(jnp.bfloat16)
        return (result[:PRE_LEN], result[PRE_LEN])
    pre_out, dec_out = lax.map(one_slot, (pre_tokens.reshape(NDEC, PRE_LEN, D), dec_tokens, req_of))
    return (pre_out.reshape(PRE_ROWS, D), dec_out)
```

```python
import functools
import math

import jax
import jax.numpy as jnp
from jax import lax
from jax.experimental import pallas as pl
from jax.experimental.pallas import tpu as pltpu
from jax.sharding import PartitionSpec as P

MESH = pl.DeviceIdType.MESH
HD = 64
EPS = 1e-05
NEG = -1e30
F32 = jnp.float32
BF16 = jnp.bfloat16
TILE = 16


def dot(a, b, ca=1, cb=0):
    return lax.dot_general(a, b, (((ca,), (cb,)), ((), ())), preferred_element_type=F32)


def norm(total, gain, shift):
    mean = jnp.mean(total, axis=-1, keepdims=True)
    centered = total - mean
    var = jnp.mean(centered * centered, axis=-1, keepdims=True)
    return centered * lax.rsqrt(var + EPS) * gain + shift


def iota(shape, dim):
    return lax.broadcasted_iota(jnp.int32, shape, dim)


def kernel(
    pre_hbm, dec_hbm, req_hbm, table_hbm, place_hbm, len_hbm, keys_hbm, values_hbm,
    wqkv_hbm, wout_hbm, g1_hbm, b1_hbm, wup_hbm, wdown_hbm, g2_hbm, b2_hbm,
    pre_out, dec_out,
    x, ctx, first, wqkv, wout, wup, wdown, keys, values,
    dec_in, req, table, place, lens, g1, b1, g2, b2,
    q_all, partial, partial_all, acc, stage, from_pair, to_chip, from_chip, result, dec_term,
    local_sem, small_sem,
    x_send, x_recv, d_send, d_recv, c_send, c_recv, e_send, e_recv, w_send, w_recv,
    q_send, q_recv, p_send, p_recv, a_send, a_recv, b_send, b_recv, t_send, t_recv, o_send, o_recv,
    *, n_req, n_tensor,
):
    rows = pre_hbm.shape[0]
    cols = pre_hbm.shape[1]
    width = cols * n_tensor
    pages = keys_hbm.shape[0] // 128
    n_chip = n_tensor // 2
    share = rows // n_tensor
    me = lax.axis_index("req")
    t = lax.axis_index("tensor")
    chip = t // 2
    core = lax.rem(t, 2)
    sib = t + 1 - 2 * core

    def on_chip(k, c):
        return lax.rem(chip + k, n_chip) * 2 + c

    def send(src, dst, ss, rs, dev):
        return pltpu.make_async_remote_copy(
            src_ref=src, dst_ref=dst, send_sem=ss, recv_sem=rs, device_id=dev, device_id_type=MESH
        )

    loads = [
        (dec_hbm, dec_in), (place_hbm, place), (table_hbm, table), (req_hbm, req), (len_hbm, lens),
        (g1_hbm, g1), (b1_hbm, b1), (g2_hbm, g2), (b2_hbm, b2),
    ]
    small = [pltpu.make_async_copy(a, b, small_sem.at[i]) for i, (a, b) in enumerate(loads)]
    for copy in small:
        copy.start()

    def own_cols(ref, lo, n):
        return ref.at[pl.ds(lo, n), pl.ds(pl.multiple_of(t * cols, cols), cols)]

    def cols_of(ref, lo, n, who):
        return ref.at[pl.ds(lo, n), pl.ds(pl.multiple_of(who * cols, cols), cols)]

    big = [
        pltpu.make_async_copy(wqkv_hbm, wqkv, local_sem.at[0]),
        pltpu.make_async_copy(pre_hbm, own_cols(x, 0, rows), local_sem.at[1]),
        pltpu.make_async_copy(keys_hbm, keys, local_sem.at[2]),
        pltpu.make_async_copy(values_hbm, values, local_sem.at[3]),
        pltpu.make_async_copy(
            wout_hbm, wout.at[pl.ds(pl.multiple_of(t * cols, cols), cols), :], local_sem.at[4]
        ),
        pltpu.make_async_copy(wup_hbm, wup, local_sem.at[5]),
        pltpu.make_async_copy(wdown_hbm, wdown, local_sem.at[6]),
    ]
    for copy in big:
        copy.start()

    barrier = pltpu.get_barrier_semaphore()
    for d in range(1, n_tensor):
        pl.semaphore_signal(
            barrier, inc=1, device_id={"tensor": lax.rem(t + d, n_tensor)}, device_id_type=MESH
        )

    def greet(k, carry):
        pl.semaphore_signal(
            barrier, inc=1, device_id={"req": lax.rem(me + k, n_req)}, device_id_type=MESH
        )
        return carry

    lax.fori_loop(1, n_req, greet, 0)

    small[0].wait()
    tile = jnp.broadcast_to(dec_in[...].astype(F32), (TILE, cols)).astype(BF16)
    own_cols(x, rows, TILE)[...] = tile

    pl.semaphore_wait(barrier, n_tensor - 1 + n_req - 1)

    def tile_exchange(ref, ss, rs):
        out = []
        for d in range(1, n_tensor):
            copy = send(
                own_cols(ref, rows, TILE), own_cols(ref, rows, TILE), ss.at[d - 1], rs.at[d - 1],
                {"tensor": lax.rem(t + d, n_tensor)},
            )
            copy.start()
            out.append(copy)
        return out

    def tile_arrival(ref, ss, rs):
        for d in range(1, n_tensor):
            part = cols_of(ref, rows, TILE, lax.rem(t - d + n_tensor, n_tensor))
            send(part, part, ss.at[d - 1], rs.at[d - 1], {"tensor": sib}).wait_recv()

    def gather_start(own, region, ss, rs):
        out = []
        for k in range(1, n_chip):
            copy = send(own, region(t), ss.at[k], rs.at[k], {"tensor": on_chip(k, core)})
            copy.start()
            out.append(copy)
        copy = send(own, region(t), ss.at[0], rs.at[0], {"tensor": sib})
        copy.start()
        out.append(copy)
        return out

    def gather_forward(region, ss, rs):
        out = []
        for k in range(1, n_chip):
            part = region(on_chip(n_chip - k, core))
            send(part, part, ss.at[k], rs.at[k], {"tensor": sib}).wait_recv()
            copy = send(part, part, ss.at[n_chip - 1 + k], rs.at[n_chip - 1 + k], {"tensor": sib})
            copy.start()
            out.append(copy)
        return out

    def gather_end(region, ss, rs):
        part = region(sib)
        send(part, part, ss.at[0], rs.at[0], {"tensor": sib}).wait_recv()
        for k in range(1, n_chip):
            part = region(on_chip(n_chip - k, 1 - core))
            send(part, part, ss.at[n_chip - 1 + k], rs.at[n_chip - 1 + k], {"tensor": sib}).wait_recv()

    def x_region(who):
        return cols_of(x, 0, rows, who)

    def c_region(who):
        return cols_of(ctx, 0, rows, who)

    def w_region(who):
        return wout.at[pl.ds(pl.multiple_of(who * cols, cols), cols), :]

    pending = tile_exchange(x, d_send, d_recv)
    pending += gather_start(pre_hbm, x_region, x_send, x_recv)

    for copy in small[1:]:
        copy.wait()
    n_page_ids = place.shape[0]
    n_r = req.shape[0]
    place_row = place[...].reshape(1, n_page_ids)
    held = place_row == (iota((TILE, n_page_ids), 0) + me * pages)
    page_id = jnp.sum(
        jnp.where(held, iota((TILE, n_page_ids), 1).astype(F32), 0.0), axis=1, keepdims=True
    )
    ids = table[...].astype(F32)
    in_page = jnp.clip(
        lens[...].reshape(1, n_r) - 128 * iota(table.shape, 0), 0, 128
    ).astype(F32)
    sub = iota((TILE, n_r), 0)
    tokens = jnp.zeros((TILE, n_r), F32)
    for s in range(pages):
        hit = jnp.sum(
            jnp.where(ids == page_id[s : s + 1, 0:1], in_page, 0.0), axis=0, keepdims=True
        )
        tokens = tokens + jnp.where(sub == s, hit, 0.0)
    req_row = jnp.broadcast_to(req[...].reshape(1, n_r).astype(F32), (8, n_r))
    lane_slot = lax.rem(iota((n_r, 2 * n_r), 1), n_r)
    twice = (iota((n_r, 2 * n_r), 0) == lane_slot).astype(F32).astype(BF16)
    req_twice = dot(req_row.astype(BF16), twice)[0:1, :]
    pick = (iota((n_r, 2 * n_r), 0).astype(F32) == req_twice).astype(F32).astype(BF16)
    in_slot = dot(tokens.astype(BF16), pick)

    lane = iota((1, cols), 1)
    low_head = lane < HD
    big[0].wait()
    tile_arrival(x, d_send, d_recv)
    x_dec = x[pl.ds(rows, TILE), :]
    q_dec = dot(x_dec, wqkv[0]).astype(BF16).astype(F32)[0:1, :]
    k_dec = dot(x_dec, wqkv[1]).astype(BF16).astype(F32)[0:1, :]
    v_dec = dot(x_dec, wqkv[2]).astype(BF16).astype(F32)[0:1, :]
    q_all[pl.ds(me, 1)] = q_dec.reshape(1, 1, cols)

    def q_copy(k):
        return send(
            q_all.at[me], q_all.at[me], q_send, q_recv, {"req": lax.rem(me + k, n_req)}
        )

    def q_start(k, carry):
        q_copy(k).start()
        return carry

    lax.fori_loop(1, n_req, q_start, 0)

    pending += gather_forward(x_region, x_send, x_recv)
    pending += gather_start(wout_hbm, w_region, w_send, w_recv)
    gather_end(x_region, x_send, x_recv)
    big[1].wait()
    x_pre = x[pl.ds(0, rows), :]
    q = dot(x_pre, wqkv[0])
    k = dot(x_pre, wqkv[1]).astype(BF16)
    v = dot(x_pre, wqkv[2]).astype(BF16)
    scale = 1.0 / math.sqrt(HD)
    causal = iota((rows, rows), 0) >= iota((rows, rows), 1)
    heads = []
    for h in range(2):
        qh = jnp.where(low_head if h == 0 else ~low_head, q, 0.0).astype(BF16)
        scores = jnp.where(causal, dot(qh, k, 1, 1) * scale, NEG)
        top = jnp.max(scores, axis=-1, keepdims=True)
        weights = jnp.where(causal, jnp.exp(scores - top), 0.0)
        total = jnp.sum(weights, axis=-1, keepdims=True)
        heads.append(dot(weights.astype(BF16), v) / total)
    own_cols(ctx, 0, rows)[...] = jnp.where(low_head, heads[0], heads[1]).astype(BF16)
    pending += gather_start(own_cols(ctx, 0, rows), c_region, c_send, c_recv)

    def q_wait(ref, sem):
        pltpu.make_async_copy(ref, ref, sem).wait()

    q_wait(q_all.at[pl.ds(0, n_req - 1)], q_recv)
    q_slots = q_all[:, 0, :]
    both = jnp.concatenate(
        [jnp.where(low_head, q_slots, 0.0), jnp.where(low_head, 0.0, q_slots)], axis=0
    ).astype(BF16)
    big[2].wait()
    big[3].wait()
    scores = dot(keys[...], both, 1, 1) * scale
    row_in_page = iota((128, 2 * n_req), 0).astype(F32)
    masks = [row_in_page < in_slot[s : s + 1, :] for s in range(pages)]
    parts = [
        jnp.where(masks[s], scores[s * 128 : (s + 1) * 128], NEG) for s in range(pages)
    ]
    top = functools.reduce(jnp.maximum, parts)
    top = jnp.max(top, axis=0, keepdims=True)
    parts = [jnp.where(m, jnp.exp(p - top), 0.0) for m, p in zip(masks, parts)]
    total = jnp.sum(functools.reduce(jnp.add, parts), axis=0, keepdims=True)
    weights = jnp.concatenate(parts, axis=0).astype(BF16)
    summed = dot(weights, values[...], 0, 0)
    diag = iota((2 * n_req, 2 * n_req), 0) == iota((2 * n_req, 2 * n_req), 1)

    def per_slot(row):
        column = jnp.sum(jnp.where(diag, row, 0.0), axis=1, keepdims=True)
        return jnp.where(low_head, column[:n_req], column[n_req:])

    first_half = lax.rem(lane, HD) < HD // 2
    partial[:, 0, :] = jnp.where(low_head, summed[:n_req], summed[n_req:])
    partial[:, 1, :] = jnp.where(first_half, per_slot(top), per_slot(total))
    partial_all[pl.ds(me, 1)] = partial[pl.ds(me, 1)]

    def p_start(k, carry):
        to = lax.rem(me + k, n_req)
        send(partial.at[to], partial_all.at[me], p_send, p_recv, {"req": to}).start()
        return carry

    lax.fori_loop(1, n_req, p_start, 0)
    pending += gather_forward(c_region, c_send, c_recv)
    pending += gather_forward(w_region, w_send, w_recv)

    q_wait(partial_all.at[pl.ds(0, n_req - 1)], p_recv)
    sums = partial_all[:, 0, :]
    stats = partial_all[:, 1, :]
    tops = jnp.where(first_half, stats, pltpu.roll(stats, HD // 2, 1))
    totals = jnp.where(first_half, pltpu.roll(stats, cols - HD // 2, 1), stats)
    qk = q_dec * k_dec
    own_score = scale * jnp.where(
        low_head,
        jnp.sum(jnp.where(low_head, qk, 0.0), axis=1, keepdims=True),
        jnp.sum(jnp.where(low_head, 0.0, qk), axis=1, keepdims=True),
    )
    best = jnp.maximum(jnp.max(tops, axis=0, keepdims=True), own_score)
    factor = jnp.exp(tops - best)
    own_weight = jnp.exp(own_score - best)
    dec_total = jnp.sum(totals * factor, axis=0, keepdims=True) + own_weight
    dec_sum = jnp.sum(sums * factor, axis=0, keepdims=True) + own_weight * v_dec
    own_cols(ctx, rows, TILE)[...] = jnp.broadcast_to(dec_sum / dec_total, (TILE, cols)).astype(BF16)
    pending += tile_exchange(ctx, e_send, e_recv)

    big[4].wait()
    gather_end(w_region, w_send, w_recv)
    gather_end(c_region, c_send, c_recv)
    tile_arrival(ctx, e_send, e_recv)
    acc[...] = dot(ctx[...], wout[...])
    gain1 = g1[...].reshape(1, width)
    shift1 = b1[...].reshape(1, width)
    for lo, n in [(0, 64), (64, 64), (128, 64), (192, 64), (256, TILE)]:
        total = x[pl.ds(lo, n), :].astype(F32) + acc[pl.ds(lo, n), :]
        first[pl.ds(lo, n), :] = norm(total, gain1, shift1).astype(BF16)
    big[5].wait()
    up = dot(first[...], wup[...])
    hidden = (0.5 * up * (1.0 + lax.erf(up * (1.0 / math.sqrt(2.0))))).astype(BF16)
    big[6].wait()
    acc[...] = dot(hidden, wdown[...])
    stage[...] = acc[pl.ds(0, rows), :].astype(BF16)
    dec_term[pl.ds(t, 1)] = acc[pl.ds(rows, 1), :].astype(BF16).astype(F32).reshape(1, 1, width)

    def rows_of(who):
        return pl.ds(pl.multiple_of(who * share, share), share)

    for k in range(n_chip):
        to = on_chip(k, 1 - core)
        copy = send(stage.at[rows_of(to), :], from_pair.at[k], a_send.at[k], a_recv.at[k], {"tensor": sib})
        copy.start()
        pending.append(copy)
    for d in range(1, n_tensor):
        copy = send(
            dec_term.at[t], dec_term.at[t], t_send.at[d - 1], t_recv.at[d - 1],
            {"tensor": lax.rem(t + d, n_tensor)},
        )
        copy.start()
        pending.append(copy)
    for k in list(range(1, n_chip)) + [0]:
        to = on_chip(k, core)
        send(stage.at[rows_of(to), :], from_pair.at[k], a_send.at[k], a_recv.at[k], {"tensor": sib}).wait_recv()
        pair = stage[rows_of(to), :].astype(F32) + from_pair[k].astype(F32)
        if k:
            to_chip[k - 1] = pair.astype(BF16)
            copy = send(
                to_chip.at[k - 1], from_chip.at[k - 1], b_send.at[k - 1], b_recv.at[k - 1], {"tensor": to}
            )
            copy.start()
            pending.append(copy)

    gain2 = g2[...].reshape(1, width)
    shift2 = b2[...].reshape(1, width)
    for d in range(1, n_tensor):
        part = dec_term.at[lax.rem(t - d + n_tensor, n_tensor)]
        send(part, part, t_send.at[d - 1], t_recv.at[d - 1], {"tensor": sib}).wait_recv()
    dec_y = first[pl.ds(rows, TILE), :].astype(F32)[0:1, :] + jnp.sum(dec_term[:, 0, :], axis=0, keepdims=True)
    acc[pl.ds(rows, 8), :] = jnp.broadcast_to(norm(dec_y, gain2, shift2), (8, width))
    dec_out[...] = acc[pl.ds(rows, 8), pl.ds(pl.multiple_of(t * cols, cols), cols)][0:1, :].astype(BF16)

    y = pair + first[rows_of(t), :].astype(F32)
    for k in range(1, n_chip):
        send(
            to_chip.at[k - 1], from_chip.at[k - 1], b_send.at[k - 1], b_recv.at[k - 1], {"tensor": sib}
        ).wait_recv()
        y = y + from_chip[k - 1].astype(F32)
    result[...] = norm(y, gain2, shift2).astype(BF16)
    pre_out[rows_of(t), :] = result[:, pl.ds(pl.multiple_of(t * cols, cols), cols)]
    for d in range(1, n_tensor):
        to = lax.rem(t + d, n_tensor)
        copy = send(
            result.at[:, pl.ds(pl.multiple_of(to * cols, cols), cols)], pre_out.at[rows_of(t), :],
            o_send.at[d - 1], o_recv.at[d - 1], {"tensor": to},
        )
        copy.start()
        pending.append(copy)
    for d in range(1, n_tensor):
        part = pre_out.at[rows_of(lax.rem(t - d + n_tensor, n_tensor)), :]
        send(part, part, o_send.at[d - 1], o_recv.at[d - 1], {"tensor": sib}).wait_recv()

    q_wait(q_all.at[pl.ds(0, n_req - 1)], q_send)
    q_wait(partial.at[pl.ds(0, n_req - 1)], p_send)
    for copy in pending:
        copy.wait_send()


def local(
    pre_tokens, dec_tokens, req_of, page_table, page_place, cache_lengths, cache_keys, cache_values,
    w_qkv, w_out, ln1_gain, ln1_bias, w_up, w_down, ln2_gain, ln2_bias,
    *, n_req, n_tensor,
):
    rows, cols = pre_tokens.shape
    width = w_qkv.shape[0]
    hidden = w_up.shape[1]
    n_keys = cache_keys.shape[0] * cache_keys.shape[1]
    share = rows // n_tensor
    n_chip = n_tensor // 2
    args = (
        pre_tokens, dec_tokens, req_of, page_table.T, page_place, cache_lengths,
        cache_keys.reshape(n_keys, cols), cache_values.reshape(n_keys, cols),
        jnp.transpose(w_qkv, (1, 0, 2)), w_out, ln1_gain, ln1_bias, w_up, w_down, ln2_gain, ln2_bias,
    )
    sem = pltpu.SemaphoreType.DMA
    vm = pltpu.VMEM
    scratch = [
        vm((rows + TILE, width), BF16),
        vm((rows + TILE, width), BF16),
        vm((rows + TILE, width), BF16),
        vm((3, width, cols), BF16),
        vm((width, width), BF16),
        vm((width, hidden), BF16),
        vm((hidden, width), BF16),
        vm((n_keys, cols), BF16),
        vm((n_keys, cols), BF16),
        vm((1, cols), BF16),
        vm(req_of.shape, jnp.int32),
        vm(page_table.shape[::-1], jnp.int32),
        vm(page_place.shape, jnp.int32),
        vm(cache_lengths.shape, jnp.int32),
        vm((width,), F32), vm((width,), F32), vm((width,), F32), vm((width,), F32),
        vm((n_req, 1, cols), F32),
        vm((n_req, 2, cols), F32),
        vm((n_req, 2, cols), F32),
        vm((rows + TILE, width), F32),
        vm((rows, width), BF16),
        vm((n_chip, share, width), BF16),
        vm((n_chip - 1, share, width), BF16),
        vm((n_chip - 1, share, width), BF16),
        vm((share, width), BF16),
        vm((n_tensor, 1, width), F32),
        sem((7,)), sem((9,)),
        sem((7,)), sem((7,)), sem((7,)), sem((7,)), sem((7,)), sem((7,)), sem((7,)), sem((7,)),
        sem((7,)), sem((7,)),
        sem, sem, sem, sem,
        sem((4,)), sem((4,)), sem((3,)), sem((3,)), sem((7,)), sem((7,)), sem((7,)), sem((7,)),
    ]
    return pl.pallas_call(
        functools.partial(kernel, n_req=n_req, n_tensor=n_tensor),
        out_shape=(
            jax.ShapeDtypeStruct((rows, cols), BF16),
            jax.ShapeDtypeStruct((1, cols), BF16),
        ),
        in_specs=[pl.BlockSpec(memory_space=pltpu.HBM)] * len(args),
        out_specs=(
            pl.BlockSpec(memory_space=pltpu.VMEM),
            pl.BlockSpec(memory_space=pltpu.VMEM),
        ),
        scratch_shapes=scratch,
        compiler_params=pltpu.CompilerParams(
            collective_id=0, has_side_effects=True, vmem_limit_bytes=56 << 20
        ),
        name="layer",
    )(*args)


def solution(mesh):
    in_specs = (
        P("req", "tensor"),
        P("req", "tensor"),
        P(),
        P(),
        P(),
        P(),
        P("req", None, "tensor"),
        P("req", None, "tensor"),
        P(None, None, "tensor"),
        P("tensor", None),
        P(),
        P(),
        P(None, "tensor"),
        P("tensor", None),
        P(),
        P(),
    )
    out_specs = (P("req", "tensor"), P("req", "tensor"))
    body = functools.partial(local, n_req=mesh.shape["req"], n_tensor=mesh.shape["tensor"])
    return jax.shard_map(body, mesh=mesh, in_specs=in_specs, out_specs=out_specs, check_vma=False)
```

```python
import functools
import math

import jax
import jax.numpy as jnp
from jax import lax
from jax.experimental import pallas as pl
from jax.experimental.pallas import tpu as pltpu
from jax.sharding import PartitionSpec as P

MESH = pl.DeviceIdType.MESH
HD = 64
EPS = 1e-05
NEG = -1e30
F32 = jnp.float32
BF16 = jnp.bfloat16
TILE = 16


def dot(a, b, ca=1, cb=0):
    return lax.dot_general(a, b, (((ca,), (cb,)), ((), ())), preferred_element_type=F32)


def norm(total, gain, shift):
    mean = jnp.mean(total, axis=-1, keepdims=True)
    centered = total - mean
    var = jnp.mean(centered * centered, axis=-1, keepdims=True)
    return centered * lax.rsqrt(var + EPS) * gain + shift


def iota(shape, dim):
    return lax.broadcasted_iota(jnp.int32, shape, dim)


def kernel(
    pre_hbm, dec_hbm, req_hbm, table_hbm, place_hbm, len_hbm, keys_hbm, values_hbm,
    wqkv_hbm, wout_hbm, g1_hbm, b1_hbm, wup_hbm, wdown_hbm, g2_hbm, b2_hbm,
    pre_out, dec_out,
    x, ctx, first, wqkv, wout, wup, wdown, keys, values,
    dec_in, req, table, place, lens, g1, b1, g2, b2,
    q_all, partial, partial_all, acc, stage, from_pair, to_chip, from_chip, result, dec_term,
    local_sem, small_sem,
    x_send, x_recv, d_send, d_recv, c_send, c_recv, e_send, e_recv, w_send, w_recv,
    q_send, q_recv, p_send, p_recv, a_send, a_recv, b_send, b_recv, t_send, t_recv, o_send, o_recv,
    *, n_req, n_tensor,
):
    rows = pre_hbm.shape[0]
    cols = pre_hbm.shape[1]
    width = cols * n_tensor
    pages = keys_hbm.shape[0] // 128
    n_chip = n_tensor // 2
    share = rows // n_tensor
    me = lax.axis_index("req")
    t = lax.axis_index("tensor")
    chip = t // 2
    core = lax.rem(t, 2)
    sib = t + 1 - 2 * core

    def on_chip(k, c):
        return lax.rem(chip + k, n_chip) * 2 + c

    def send(src, dst, ss, rs, dev):
        return pltpu.make_async_remote_copy(
            src_ref=src, dst_ref=dst, send_sem=ss, recv_sem=rs, device_id=dev, device_id_type=MESH
        )

    loads = [
        (dec_hbm, dec_in), (place_hbm, place), (table_hbm, table), (req_hbm, req), (len_hbm, lens),
        (g1_hbm, g1), (b1_hbm, b1), (g2_hbm, g2), (b2_hbm, b2),
    ]
    small = [pltpu.make_async_copy(a, b, small_sem.at[i]) for i, (a, b) in enumerate(loads)]
    for copy in small:
        copy.start()

    def own_cols(ref, lo, n):
        return ref.at[pl.ds(lo, n), pl.ds(pl.multiple_of(t * cols, cols), cols)]

    def cols_of(ref, lo, n, who):
        return ref.at[pl.ds(lo, n), pl.ds(pl.multiple_of(who * cols, cols), cols)]

    big = [
        pltpu.make_async_copy(wqkv_hbm, wqkv, local_sem.at[0]),
        pltpu.make_async_copy(pre_hbm, own_cols(x, 0, rows), local_sem.at[1]),
        pltpu.make_async_copy(keys_hbm, keys, local_sem.at[2]),
        pltpu.make_async_copy(values_hbm, values, local_sem.at[3]),
        pltpu.make_async_copy(
            wout_hbm, wout.at[pl.ds(pl.multiple_of(t * cols, cols), cols), :], local_sem.at[4]
        ),
        pltpu.make_async_copy(wup_hbm, wup, local_sem.at[5]),
        pltpu.make_async_copy(wdown_hbm, wdown, local_sem.at[6]),
    ]
    for copy in big:
        copy.start()

    barrier = pltpu.get_barrier_semaphore()
    for d in range(1, n_tensor):
        pl.semaphore_signal(
            barrier, inc=1, device_id={"tensor": lax.rem(t + d, n_tensor)}, device_id_type=MESH
        )

    def each_peer(visit):
        group = 9 if (n_req - 1) % 9 == 0 else 1

        def some(i, carry):
            for j in range(group):
                visit(lax.rem(me + 1 + i * group + j, n_req))
            return carry

        lax.fori_loop(0, (n_req - 1) // group, some, 0)

    each_peer(
        lambda to: pl.semaphore_signal(barrier, inc=1, device_id={"req": to}, device_id_type=MESH)
    )

    pending = []
    small[0].wait()
    tile = jnp.broadcast_to(dec_in[...].astype(F32), (TILE, cols)).astype(BF16)
    own_cols(x, rows, TILE)[...] = tile

    pl.semaphore_wait(barrier, n_tensor - 1 + n_req - 1)

    def tile_exchange(ref, ss, rs):
        out = []
        for d in range(1, n_tensor):
            copy = send(
                own_cols(ref, rows, TILE), own_cols(ref, rows, TILE), ss.at[d - 1], rs.at[d - 1],
                {"tensor": lax.rem(t + d, n_tensor)},
            )
            copy.start()
            out.append(copy)
        return out

    def tile_arrival(ref, ss, rs):
        for d in range(1, n_tensor):
            part = cols_of(ref, rows, TILE, lax.rem(t - d + n_tensor, n_tensor))
            send(part, part, ss.at[d - 1], rs.at[d - 1], {"tensor": sib}).wait_recv()

    def gather(own, region, ss, rs):
        def go(i, src, dst, dev):
            copy = send(src, dst, ss.at[i], rs.at[i], {"tensor": dev})
            copy.start()
            pending.append(copy)

        def arrived(i, ref):
            send(ref, ref, ss.at[i], rs.at[i], {"tensor": sib}).wait_recv()

        def begin():
            for k in (2, 1, 3):
                go(k, own, region(t), on_chip(k, core))
            go(0, own, region(t), sib)

        def forward():
            for k in (1, 3, 2):
                part = region(on_chip(n_chip - k, core))
                arrived(k, part)
                go(3 + k, part, part, sib)

        def end():
            arrived(0, region(sib))
            for k in (1, 3, 2):
                arrived(3 + k, region(on_chip(n_chip - k, 1 - core)))

        return begin, forward, end

    def x_region(who):
        return cols_of(x, 0, rows, who)

    def c_region(who):
        return cols_of(ctx, 0, rows, who)

    def w_region(who):
        return wout.at[pl.ds(pl.multiple_of(who * cols, cols), cols), :]

    gather_x = gather(pre_hbm, x_region, x_send, x_recv)
    gather_w = gather(wout_hbm, w_region, w_send, w_recv)
    gather_c = gather(own_cols(ctx, 0, rows), c_region, c_send, c_recv)

    pending += tile_exchange(x, d_send, d_recv)
    gather_x[0]()
    gather_w[0]()

    lane = iota((1, cols), 1)
    low_head = lane < HD
    big[0].wait()
    tile_arrival(x, d_send, d_recv)
    x_dec = x[pl.ds(rows, TILE), :]
    q_dec = dot(x_dec, wqkv[0]).astype(BF16).astype(F32)[0:1, :]
    q_all[pl.ds(me, 1)] = q_dec.reshape(1, 1, cols)
    each_peer(lambda to: send(q_all.at[me], q_all.at[me], q_send, q_recv, {"req": to}).start())
    k_dec = dot(x_dec, wqkv[1]).astype(BF16).astype(F32)[0:1, :]
    v_dec = dot(x_dec, wqkv[2]).astype(BF16).astype(F32)[0:1, :]

    gather_x[1]()
    for copy in small[1:]:
        copy.wait()
    n_page_ids = place.shape[0]
    n_r = req.shape[0]
    place_row = place[...].reshape(1, n_page_ids)
    held = place_row == (iota((TILE, n_page_ids), 0) + me * pages)
    page_id = jnp.sum(
        jnp.where(held, iota((TILE, n_page_ids), 1).astype(F32), 0.0), axis=1, keepdims=True
    )
    ids = table[...].astype(F32)
    in_page = jnp.clip(
        lens[...].reshape(1, n_r) - 128 * iota(table.shape, 0), 0, 128
    ).astype(F32)
    sub = iota((TILE, n_r), 0)
    tokens = jnp.zeros((TILE, n_r), F32)
    for s in range(pages):
        hit = jnp.sum(
            jnp.where(ids == page_id[s : s + 1, 0:1], in_page, 0.0), axis=0, keepdims=True
        )
        tokens = tokens + jnp.where(sub == s, hit, 0.0)
    req_row = jnp.broadcast_to(req[...].reshape(1, n_r).astype(F32), (8, n_r))
    lane_slot = lax.rem(iota((n_r, 2 * n_r), 1), n_r)
    twice = (iota((n_r, 2 * n_r), 0) == lane_slot).astype(F32).astype(BF16)
    req_twice = dot(req_row.astype(BF16), twice)[0:1, :]
    pick = (iota((n_r, 2 * n_r), 0).astype(F32) == req_twice).astype(F32).astype(BF16)
    in_slot = dot(tokens.astype(BF16), pick)

    gather_x[2]()
    big[1].wait()
    x_pre = x[pl.ds(0, rows), :]
    q = dot(x_pre, wqkv[0])
    k = dot(x_pre, wqkv[1]).astype(BF16)
    v = dot(x_pre, wqkv[2]).astype(BF16)
    scale = 1.0 / math.sqrt(HD)
    causal = iota((rows, rows), 0) >= iota((rows, rows), 1)
    heads = []
    for h in range(2):
        qh = jnp.where(low_head if h == 0 else ~low_head, q, 0.0).astype(BF16)
        scores = jnp.where(causal, dot(qh, k, 1, 1) * scale, NEG)
        top = jnp.max(scores, axis=-1, keepdims=True)
        weights = jnp.where(causal, jnp.exp(scores - top), 0.0)
        total = jnp.sum(weights, axis=-1, keepdims=True)
        heads.append(dot(weights.astype(BF16), v) / total)
    own_cols(ctx, 0, rows)[...] = jnp.where(low_head, heads[0], heads[1]).astype(BF16)
    gather_c[0]()

    def q_wait(ref, sem):
        pltpu.make_async_copy(ref, ref, sem).wait()

    big[2].wait()
    big[3].wait()
    q_wait(q_all.at[pl.ds(0, n_req - 1)], q_recv)
    q_slots = q_all[:, 0, :]
    both = jnp.concatenate(
        [jnp.where(low_head, q_slots, 0.0), jnp.where(low_head, 0.0, q_slots)], axis=0
    ).astype(BF16)
    scores = dot(keys[...], both, 1, 1) * scale
    row_in_page = iota((128, 2 * n_req), 0).astype(F32)
    masks = [row_in_page < in_slot[s : s + 1, :] for s in range(pages)]
    parts = [
        jnp.where(masks[s], scores[s * 128 : (s + 1) * 128], NEG) for s in range(pages)
    ]
    top = functools.reduce(jnp.maximum, parts)
    top = jnp.max(top, axis=0, keepdims=True)
    parts = [jnp.where(m, jnp.exp(p - top), 0.0) for m, p in zip(masks, parts)]
    total = jnp.sum(functools.reduce(jnp.add, parts), axis=0, keepdims=True)
    weights = jnp.concatenate(parts, axis=0).astype(BF16)
    summed = dot(weights, values[...], 0, 0)
    diag = iota((2 * n_req, 2 * n_req), 0) == iota((2 * n_req, 2 * n_req), 1)

    def per_slot(row):
        column = jnp.sum(jnp.where(diag, row, 0.0), axis=1, keepdims=True)
        return jnp.where(low_head, column[:n_req], column[n_req:])

    first_half = lax.rem(lane, HD) < HD // 2
    partial[:, 0, :] = jnp.where(low_head, summed[:n_req], summed[n_req:])
    partial[:, 1, :] = jnp.where(first_half, per_slot(top), per_slot(total))
    partial_all[pl.ds(me, 1)] = partial[pl.ds(me, 1)]
    each_peer(lambda to: send(partial.at[to], partial_all.at[me], p_send, p_recv, {"req": to}).start())

    gather_c[1]()
    gather_w[1]()
    gain1 = g1[...].reshape(1, width)
    shift1 = b1[...].reshape(1, width)
    gain2 = g2[...].reshape(1, width)
    shift2 = b2[...].reshape(1, width)

    def feed_forward(lo, n, chunk):
        acc[pl.ds(lo, n), :] = dot(ctx[pl.ds(lo, n), :], wout[...])
        for at in range(lo, lo + n, chunk):
            total = x[pl.ds(at, chunk), :].astype(F32) + acc[pl.ds(at, chunk), :]
            first[pl.ds(at, chunk), :] = norm(total, gain1, shift1).astype(BF16)
        up = dot(first[pl.ds(lo, n), :], wup[...])
        hidden = (0.5 * up * (1.0 + lax.erf(up * (1.0 / math.sqrt(2.0))))).astype(BF16)
        return dot(hidden, wdown[...])

    big[4].wait()
    big[5].wait()
    big[6].wait()
    gather_c[2]()
    gather_w[2]()
    stage[...] = feed_forward(0, rows, 64).astype(BF16)

    def rows_of(who):
        return pl.ds(pl.multiple_of(who * share, share), share)

    for k in range(n_chip):
        to = on_chip(k, 1 - core)
        copy = send(stage.at[rows_of(to), :], from_pair.at[k], a_send.at[k], a_recv.at[k], {"tensor": sib})
        copy.start()
        pending.append(copy)
    for k in (2, 1, 3, 0):
        to = on_chip(k, core)
        send(stage.at[rows_of(to), :], from_pair.at[k], a_send.at[k], a_recv.at[k], {"tensor": sib}).wait_recv()
        pair = stage[rows_of(to), :].astype(F32) + from_pair[k].astype(F32)
        if k:
            to_chip[k - 1] = pair.astype(BF16)
            copy = send(
                to_chip.at[k - 1], from_chip.at[k - 1], b_send.at[k - 1], b_recv.at[k - 1], {"tensor": to}
            )
            copy.start()
            pending.append(copy)

    q_wait(partial_all.at[pl.ds(0, n_req - 1)], p_recv)
    sums = partial_all[:, 0, :]
    stats = partial_all[:, 1, :]
    tops = jnp.where(first_half, stats, pltpu.roll(stats, HD // 2, 1))
    totals = jnp.where(first_half, pltpu.roll(stats, cols - HD // 2, 1), stats)
    qk = q_dec * k_dec
    own_score = scale * jnp.where(
        low_head,
        jnp.sum(jnp.where(low_head, qk, 0.0), axis=1, keepdims=True),
        jnp.sum(jnp.where(low_head, 0.0, qk), axis=1, keepdims=True),
    )
    best = jnp.maximum(jnp.max(tops, axis=0, keepdims=True), own_score)
    factor = jnp.exp(tops - best)
    own_weight = jnp.exp(own_score - best)
    dec_total = jnp.sum(totals * factor, axis=0, keepdims=True) + own_weight
    dec_sum = jnp.sum(sums * factor, axis=0, keepdims=True) + own_weight * v_dec
    own_cols(ctx, rows, TILE)[...] = jnp.broadcast_to(dec_sum / dec_total, (TILE, cols)).astype(BF16)
    pending += tile_exchange(ctx, e_send, e_recv)

    y = pair + first[rows_of(t), :].astype(F32)
    for k in (1, 3, 2):
        send(
            to_chip.at[k - 1], from_chip.at[k - 1], b_send.at[k - 1], b_recv.at[k - 1], {"tensor": sib}
        ).wait_recv()
        y = y + from_chip[k - 1].astype(F32)
    result[...] = norm(y, gain2, shift2).astype(BF16)
    pre_out[rows_of(t), :] = result[:, pl.ds(pl.multiple_of(t * cols, cols), cols)]
    for d in range(1, n_tensor):
        to = lax.rem(t + d, n_tensor)
        copy = send(
            result.at[:, pl.ds(pl.multiple_of(to * cols, cols), cols)], pre_out.at[rows_of(t), :],
            o_send.at[d - 1], o_recv.at[d - 1], {"tensor": to},
        )
        copy.start()
        pending.append(copy)

    tile_arrival(ctx, e_send, e_recv)
    term = feed_forward(rows, TILE, TILE)[0:1, :].astype(BF16).astype(F32)
    dec_term[pl.ds(t, 1)] = term.reshape(1, 1, width)
    for d in range(1, n_tensor):
        copy = send(
            dec_term.at[t], dec_term.at[t], t_send.at[d - 1], t_recv.at[d - 1],
            {"tensor": lax.rem(t + d, n_tensor)},
        )
        copy.start()
        pending.append(copy)
    q_wait(q_all.at[pl.ds(0, n_req - 1)], q_send)
    q_wait(partial.at[pl.ds(0, n_req - 1)], p_send)
    for d in range(1, n_tensor):
        part = dec_term.at[lax.rem(t - d + n_tensor, n_tensor)]
        send(part, part, t_send.at[d - 1], t_recv.at[d - 1], {"tensor": sib}).wait_recv()
    dec_y = first[pl.ds(rows, TILE), :].astype(F32)[0:1, :] + jnp.sum(dec_term[:, 0, :], axis=0, keepdims=True)
    acc[pl.ds(rows, 8), :] = jnp.broadcast_to(norm(dec_y, gain2, shift2), (8, width))
    dec_out[...] = acc[pl.ds(rows, 8), pl.ds(pl.multiple_of(t * cols, cols), cols)][0:1, :].astype(BF16)

    for d in range(1, n_tensor):
        part = pre_out.at[rows_of(lax.rem(t - d + n_tensor, n_tensor)), :]
        send(part, part, o_send.at[d - 1], o_recv.at[d - 1], {"tensor": sib}).wait_recv()
    for copy in pending:
        copy.wait_send()


def local(
    pre_tokens, dec_tokens, req_of, page_table, page_place, cache_lengths, cache_keys, cache_values,
    w_qkv, w_out, ln1_gain, ln1_bias, w_up, w_down, ln2_gain, ln2_bias,
    *, n_req, n_tensor,
):
    rows, cols = pre_tokens.shape
    width = w_qkv.shape[0]
    hidden = w_up.shape[1]
    n_keys = cache_keys.shape[0] * cache_keys.shape[1]
    share = rows // n_tensor
    n_chip = n_tensor // 2
    args = (
        pre_tokens, dec_tokens, req_of, page_table.T, page_place, cache_lengths,
        cache_keys.reshape(n_keys, cols), cache_values.reshape(n_keys, cols),
        jnp.transpose(w_qkv, (1, 0, 2)), w_out, ln1_gain, ln1_bias, w_up, w_down, ln2_gain, ln2_bias,
    )
    sem = pltpu.SemaphoreType.DMA
    vm = pltpu.VMEM
    scratch = [
        vm((rows + TILE, width), BF16),
        vm((rows + TILE, width), BF16),
        vm((rows + TILE, width), BF16),
        vm((3, width, cols), BF16),
        vm((width, width), BF16),
        vm((width, hidden), BF16),
        vm((hidden, width), BF16),
        vm((n_keys, cols), BF16),
        vm((n_keys, cols), BF16),
        vm((1, cols), BF16),
        vm(req_of.shape, jnp.int32),
        vm(page_table.shape[::-1], jnp.int32),
        vm(page_place.shape, jnp.int32),
        vm(cache_lengths.shape, jnp.int32),
        vm((width,), F32), vm((width,), F32), vm((width,), F32), vm((width,), F32),
        vm((n_req, 1, cols), F32),
        vm((n_req, 2, cols), F32),
        vm((n_req, 2, cols), F32),
        vm((rows + TILE, width), F32),
        vm((rows, width), BF16),
        vm((n_chip, share, width), BF16),
        vm((n_chip - 1, share, width), BF16),
        vm((n_chip - 1, share, width), BF16),
        vm((share, width), BF16),
        vm((n_tensor, 1, width), F32),
        sem((7,)), sem((9,)),
        sem((9,)), sem((9,)), sem((7,)), sem((7,)), sem((9,)), sem((9,)), sem((7,)), sem((7,)),
        sem((9,)), sem((9,)),
        sem, sem, sem, sem,
        sem((4,)), sem((4,)), sem((3,)), sem((3,)), sem((7,)), sem((7,)), sem((7,)), sem((7,)),
    ]
    return pl.pallas_call(
        functools.partial(kernel, n_req=n_req, n_tensor=n_tensor),
        out_shape=(
            jax.ShapeDtypeStruct((rows, cols), BF16),
            jax.ShapeDtypeStruct((1, cols), BF16),
        ),
        in_specs=[pl.BlockSpec(memory_space=pltpu.HBM)] * len(args),
        out_specs=(
            pl.BlockSpec(memory_space=pltpu.VMEM),
            pl.BlockSpec(memory_space=pltpu.VMEM),
        ),
        scratch_shapes=scratch,
        compiler_params=pltpu.CompilerParams(
            collective_id=0, has_side_effects=True, vmem_limit_bytes=56 << 20
        ),
        name="layer",
    )(*args)


def solution(mesh):
    in_specs = (
        P("req", "tensor"),
        P("req", "tensor"),
        P(),
        P(),
        P(),
        P(),
        P("req", None, "tensor"),
        P("req", None, "tensor"),
        P(None, None, "tensor"),
        P("tensor", None),
        P(),
        P(),
        P(None, "tensor"),
        P("tensor", None),
        P(),
        P(),
    )
    out_specs = (P("req", "tensor"), P("req", "tensor"))
    body = functools.partial(local, n_req=mesh.shape["req"], n_tensor=mesh.shape["tensor"])
    return jax.shard_map(body, mesh=mesh, in_specs=in_specs, out_specs=out_specs, check_vma=False)
```

```python
import functools
import math

import jax
import jax.numpy as jnp
from jax import lax
from jax.experimental import pallas as pl
from jax.experimental.pallas import tpu as pltpu
from jax.sharding import PartitionSpec as P

MESH = pl.DeviceIdType.MESH
HD = 64
EPS = 1e-05
NEG = -1e30
F32 = jnp.float32
BF16 = jnp.bfloat16
TILE = 16


def dot(a, b, ca=1, cb=0):
    return lax.dot_general(a, b, (((ca,), (cb,)), ((), ())), preferred_element_type=F32)


def norm(total, gain, shift):
    mean = jnp.mean(total, axis=-1, keepdims=True)
    centered = total - mean
    var = jnp.mean(centered * centered, axis=-1, keepdims=True)
    return centered * lax.rsqrt(var + EPS) * gain + shift


def iota(shape, dim):
    return lax.broadcasted_iota(jnp.int32, shape, dim)


def kernel(
    pre_hbm, dec_hbm, req_hbm, table_hbm, place_hbm, len_hbm, keys_hbm, values_hbm,
    wqkv_hbm, wout_hbm, g1_hbm, b1_hbm, wup_hbm, wdown_hbm, g2_hbm, b2_hbm,
    pre_out, dec_out,
    x, ctx, first, wqkv, wout, wup, wdown, keys, values,
    dec_in, req, table, place, lens, g1, b1, g2, b2,
    q_all, partial, partial_all, acc, stage, from_pair, to_chip, from_chip, result, dec_term,
    local_sem, small_sem,
    x_send, x_recv, d_send, d_recv, c_send, c_recv, e_send, e_recv, w_send, w_recv,
    q_send, q_recv, p_send, p_recv, a_send, a_recv, b_send, b_recv, t_send, t_recv, o_send, o_recv,
    *, n_req, n_tensor,
):
    rows = pre_hbm.shape[0]
    cols = pre_hbm.shape[1]
    width = cols * n_tensor
    pages = keys_hbm.shape[0] // 128
    n_chip = n_tensor // 2
    share = rows // n_tensor
    me = lax.axis_index("req")
    t = lax.axis_index("tensor")
    chip = t // 2
    core = lax.rem(t, 2)
    sib = t + 1 - 2 * core

    def on_chip(k, c):
        return lax.rem(chip + k, n_chip) * 2 + c

    def send(src, dst, ss, rs, dev):
        return pltpu.make_async_remote_copy(
            src_ref=src, dst_ref=dst, send_sem=ss, recv_sem=rs, device_id=dev, device_id_type=MESH
        )

    n_z = 16 if n_req % 16 == 0 else n_req
    n_y = n_req // n_z
    ys = sorted(range(n_y), key=lambda dy: -min(dy, n_y - dy))

    def each_peer(visit):
        my, mz = me // n_z, lax.rem(me, n_z)

        def visit_ring(dz, dys):
            for dy in dys:
                visit(lax.rem(my + dy, n_y) * n_z + lax.rem(mz + dz, n_z))

        def both_ways(i, carry):
            dz = n_z // 2 - 1 - i
            visit_ring(dz, ys)
            visit_ring(n_z - dz, ys)
            return carry

        visit_ring(n_z // 2, ys)
        lax.fori_loop(0, n_z // 2 - 1, both_ways, 0)
        visit_ring(0, [dy for dy in ys if dy])

    barrier = pltpu.get_barrier_semaphore()
    each_peer(
        lambda to: pl.semaphore_signal(barrier, inc=1, device_id={"req": to}, device_id_type=MESH)
    )
    for d in range(1, n_tensor):
        pl.semaphore_signal(
            barrier, inc=1, device_id={"tensor": lax.rem(t + d, n_tensor)}, device_id_type=MESH
        )

    loads = [
        (dec_hbm, dec_in), (place_hbm, place), (table_hbm, table), (req_hbm, req), (len_hbm, lens),
        (g1_hbm, g1), (b1_hbm, b1), (g2_hbm, g2), (b2_hbm, b2),
    ]
    small = [pltpu.make_async_copy(a, b, small_sem.at[i]) for i, (a, b) in enumerate(loads)]
    for copy in small:
        copy.start()

    def own_cols(ref, lo, n):
        return ref.at[pl.ds(lo, n), pl.ds(pl.multiple_of(t * cols, cols), cols)]

    def cols_of(ref, lo, n, who):
        return ref.at[pl.ds(lo, n), pl.ds(pl.multiple_of(who * cols, cols), cols)]

    big = [
        pltpu.make_async_copy(wqkv_hbm, wqkv, local_sem.at[0]),
        pltpu.make_async_copy(pre_hbm, own_cols(x, 0, rows), local_sem.at[1]),
        pltpu.make_async_copy(keys_hbm, keys, local_sem.at[2]),
        pltpu.make_async_copy(values_hbm, values, local_sem.at[3]),
        pltpu.make_async_copy(
            wout_hbm, wout.at[pl.ds(pl.multiple_of(t * cols, cols), cols), :], local_sem.at[4]
        ),
        pltpu.make_async_copy(wup_hbm, wup, local_sem.at[5]),
        pltpu.make_async_copy(wdown_hbm, wdown, local_sem.at[6]),
    ]
    for copy in big:
        copy.start()

    pending = []
    small[0].wait()
    tile = jnp.broadcast_to(dec_in[...].astype(F32), (TILE, cols)).astype(BF16)
    own_cols(x, rows, TILE)[...] = tile

    pl.semaphore_wait(barrier, n_tensor - 1 + n_req - 1)

    def tile_exchange(ref, ss, rs):
        out = []
        for d in sorted(range(1, n_tensor), key=lambda d: abs(d - n_tensor // 2)):
            copy = send(
                own_cols(ref, rows, TILE), own_cols(ref, rows, TILE), ss.at[d - 1], rs.at[d - 1],
                {"tensor": lax.rem(t + d, n_tensor)},
            )
            copy.start()
            out.append(copy)
        return out

    def tile_arrival(ref, ss, rs):
        for d in range(1, n_tensor):
            part = cols_of(ref, rows, TILE, lax.rem(t - d + n_tensor, n_tensor))
            send(part, part, ss.at[d - 1], rs.at[d - 1], {"tensor": sib}).wait_recv()

    def gather(own, region, ss, rs):
        def go(i, src, dst, dev):
            copy = send(src, dst, ss.at[i], rs.at[i], {"tensor": dev})
            copy.start()
            pending.append(copy)

        def arrived(i, ref):
            send(ref, ref, ss.at[i], rs.at[i], {"tensor": sib}).wait_recv()

        def begin():
            for k in (2, 1, 3):
                go(k, own, region(t), on_chip(k, core))
            go(0, own, region(t), sib)

        def forward():
            for k in (1, 3, 2):
                part = region(on_chip(n_chip - k, core))
                arrived(k, part)
                go(3 + k, part, part, sib)

        def end():
            arrived(0, region(sib))
            for k in (1, 3, 2):
                arrived(3 + k, region(on_chip(n_chip - k, 1 - core)))

        return begin, forward, end

    right, left, far = on_chip(1, core), on_chip(n_chip - 1, core), on_chip(2, core)

    def relay(own, region, ss, rs):
        def halves(who):
            ref = region(who)
            n = ref.shape[0] // 2
            return ref.at[pl.ds(0, n), :], ref.at[pl.ds(n, n), :]

        def go(i, src, dst, dev):
            copy = send(src, dst, ss.at[i], rs.at[i], {"tensor": dev})
            copy.start()
            pending.append(copy)

        def arrived(i, ref):
            send(ref, ref, ss.at[i], rs.at[i], {"tensor": sib}).wait_recv()

        def begin():
            go(1, own, region(t), right)
            go(2, own, region(t), left)
            go(0, own, region(t), sib)

        def onward():
            arrived(1, region(left))
            top, _ = halves(left)
            go(3, top, top, right)
            arrived(2, region(right))
            _, bottom = halves(right)
            go(4, bottom, bottom, left)
            go(5, region(left), region(left), sib)
            go(6, region(right), region(right), sib)

        def across():
            top, bottom = halves(far)
            arrived(3, top)
            go(7, top, top, sib)
            arrived(4, bottom)
            go(8, bottom, bottom, sib)

        def end():
            arrived(0, region(sib))
            arrived(5, region(on_chip(n_chip - 1, 1 - core)))
            arrived(6, region(on_chip(1, 1 - core)))
            top, bottom = halves(on_chip(2, 1 - core))
            arrived(7, top)
            arrived(8, bottom)

        return begin, onward, across, end

    def x_region(who):
        return cols_of(x, 0, rows, who)

    def c_region(who):
        return cols_of(ctx, 0, rows, who)

    def w_region(who):
        return wout.at[pl.ds(pl.multiple_of(who * cols, cols), cols), :]

    gather_x = gather(pre_hbm, x_region, x_send, x_recv)
    gather_w = relay(wout_hbm, w_region, w_send, w_recv)
    gather_c = gather(own_cols(ctx, 0, rows), c_region, c_send, c_recv)

    pending += tile_exchange(x, d_send, d_recv)
    gather_x[0]()
    gather_w[0]()

    lane = iota((1, cols), 1)
    low_head = lane < HD
    big[0].wait()
    tile_arrival(x, d_send, d_recv)
    x_dec = x[pl.ds(rows, TILE), :]
    q_dec = dot(x_dec, wqkv[0]).astype(BF16).astype(F32)[0:1, :]
    q_all[pl.ds(me, 1)] = q_dec.reshape(1, 1, cols)
    each_peer(lambda to: send(q_all.at[me], q_all.at[me], q_send, q_recv, {"req": to}).start())
    k_dec = dot(x_dec, wqkv[1]).astype(BF16).astype(F32)[0:1, :]
    v_dec = dot(x_dec, wqkv[2]).astype(BF16).astype(F32)[0:1, :]

    gather_x[1]()
    for copy in small[1:]:
        copy.wait()
    n_page_ids = place.shape[0]
    n_r = req.shape[0]
    place_row = place[...].reshape(1, n_page_ids)
    held = place_row == (iota((TILE, n_page_ids), 0) + me * pages)
    page_id = jnp.sum(
        jnp.where(held, iota((TILE, n_page_ids), 1).astype(F32), 0.0), axis=1, keepdims=True
    )
    ids = table[...].astype(F32)
    in_page = jnp.clip(
        lens[...].reshape(1, n_r) - 128 * iota(table.shape, 0), 0, 128
    ).astype(F32)
    sub = iota((TILE, n_r), 0)
    tokens = jnp.zeros((TILE, n_r), F32)
    for s in range(pages):
        hit = jnp.sum(
            jnp.where(ids == page_id[s : s + 1, 0:1], in_page, 0.0), axis=0, keepdims=True
        )
        tokens = tokens + jnp.where(sub == s, hit, 0.0)
    req_row = jnp.broadcast_to(req[...].reshape(1, n_r).astype(F32), (8, n_r))
    lane_slot = lax.rem(iota((n_r, 2 * n_r), 1), n_r)
    twice = (iota((n_r, 2 * n_r), 0) == lane_slot).astype(F32).astype(BF16)
    req_twice = dot(req_row.astype(BF16), twice)[0:1, :]
    pick = (iota((n_r, 2 * n_r), 0).astype(F32) == req_twice).astype(F32).astype(BF16)
    in_slot = dot(tokens.astype(BF16), pick)

    gather_x[2]()
    big[1].wait()
    x_pre = x[pl.ds(0, rows), :]
    q = dot(x_pre, wqkv[0])
    k = dot(x_pre, wqkv[1]).astype(BF16)
    v = dot(x_pre, wqkv[2]).astype(BF16)
    scale = 1.0 / math.sqrt(HD)
    causal = iota((rows, rows), 0) >= iota((rows, rows), 1)
    heads = []
    for h in range(2):
        qh = jnp.where(low_head if h == 0 else ~low_head, q, 0.0).astype(BF16)
        scores = jnp.where(causal, dot(qh, k, 1, 1) * scale, NEG)
        top = jnp.max(scores, axis=-1, keepdims=True)
        weights = jnp.where(causal, jnp.exp(scores - top), 0.0)
        total = jnp.sum(weights, axis=-1, keepdims=True)
        heads.append(dot(weights.astype(BF16), v) / total)
    own_cols(ctx, 0, rows)[...] = jnp.where(low_head, heads[0], heads[1]).astype(BF16)
    gather_c[0]()
    gather_w[1]()

    def q_wait(ref, sem):
        pltpu.make_async_copy(ref, ref, sem).wait()

    big[2].wait()
    big[3].wait()
    q_wait(q_all.at[pl.ds(0, n_req - 1)], q_recv)
    q_slots = q_all[:, 0, :]
    both = jnp.concatenate(
        [jnp.where(low_head, q_slots, 0.0), jnp.where(low_head, 0.0, q_slots)], axis=0
    ).astype(BF16)
    scores = dot(keys[...], both, 1, 1) * scale
    row_in_page = iota((128, 2 * n_req), 0).astype(F32)
    masks = [row_in_page < in_slot[s : s + 1, :] for s in range(pages)]
    parts = [
        jnp.where(masks[s], scores[s * 128 : (s + 1) * 128], NEG) for s in range(pages)
    ]
    top = functools.reduce(jnp.maximum, parts)
    top = jnp.max(top, axis=0, keepdims=True)
    parts = [jnp.where(m, jnp.exp(p - top), 0.0) for m, p in zip(masks, parts)]
    total = jnp.sum(functools.reduce(jnp.add, parts), axis=0, keepdims=True)
    weights = jnp.concatenate(parts, axis=0).astype(BF16)
    summed = dot(weights, values[...], 0, 0)
    diag = iota((2 * n_req, 2 * n_req), 0) == iota((2 * n_req, 2 * n_req), 1)

    def per_slot(row):
        column = jnp.sum(jnp.where(diag, row, 0.0), axis=1, keepdims=True)
        return jnp.where(low_head, column[:n_req], column[n_req:])

    first_half = lax.rem(lane, HD) < HD // 2
    partial[:, 0, :] = jnp.where(low_head, summed[:n_req], summed[n_req:])
    partial[:, 1, :] = jnp.where(first_half, per_slot(top), per_slot(total))
    partial_all[pl.ds(me, 1)] = partial[pl.ds(me, 1)]
    each_peer(lambda to: send(partial.at[to], partial_all.at[me], p_send, p_recv, {"req": to}).start())

    gather_c[1]()
    gather_w[2]()
    gain1 = g1[...].reshape(1, width)
    shift1 = b1[...].reshape(1, width)
    gain2 = g2[...].reshape(1, width)
    shift2 = b2[...].reshape(1, width)

    def feed_forward(lo, n, chunk):
        acc[pl.ds(lo, n), :] = dot(ctx[pl.ds(lo, n), :], wout[...])
        for at in range(lo, lo + n, chunk):
            total = x[pl.ds(at, chunk), :].astype(F32) + acc[pl.ds(at, chunk), :]
            first[pl.ds(at, chunk), :] = norm(total, gain1, shift1).astype(BF16)
        up = dot(first[pl.ds(lo, n), :], wup[...])
        hidden = (0.5 * up * (1.0 + lax.erf(up * (1.0 / math.sqrt(2.0))))).astype(BF16)
        return dot(hidden, wdown[...])

    big[4].wait()
    big[5].wait()
    big[6].wait()
    gather_c[2]()
    gather_w[3]()
    stage[...] = feed_forward(0, rows, 64).astype(BF16)

    def rows_of(who):
        return pl.ds(pl.multiple_of(who * share, share), share)

    for k in range(n_chip):
        to = on_chip(k, 1 - core)
        copy = send(stage.at[rows_of(to), :], from_pair.at[k], a_send.at[k], a_recv.at[k], {"tensor": sib})
        copy.start()
        pending.append(copy)
    for k in (2, 1, 3, 0):
        to = on_chip(k, core)
        send(stage.at[rows_of(to), :], from_pair.at[k], a_send.at[k], a_recv.at[k], {"tensor": sib}).wait_recv()
        pair = stage[rows_of(to), :].astype(F32) + from_pair[k].astype(F32)
        if k:
            to_chip[k - 1] = pair.astype(BF16)
            copy = send(
                to_chip.at[k - 1], from_chip.at[k - 1], b_send.at[k - 1], b_recv.at[k - 1], {"tensor": to}
            )
            copy.start()
            pending.append(copy)

    q_wait(partial_all.at[pl.ds(0, n_req - 1)], p_recv)
    sums = partial_all[:, 0, :]
    stats = partial_all[:, 1, :]
    tops = jnp.where(first_half, stats, pltpu.roll(stats, HD // 2, 1))
    totals = jnp.where(first_half, pltpu.roll(stats, cols - HD // 2, 1), stats)
    qk = q_dec * k_dec
    own_score = scale * jnp.where(
        low_head,
        jnp.sum(jnp.where(low_head, qk, 0.0), axis=1, keepdims=True),
        jnp.sum(jnp.where(low_head, 0.0, qk), axis=1, keepdims=True),
    )
    best = jnp.maximum(jnp.max(tops, axis=0, keepdims=True), own_score)
    factor = jnp.exp(tops - best)
    own_weight = jnp.exp(own_score - best)
    dec_total = jnp.sum(totals * factor, axis=0, keepdims=True) + own_weight
    dec_sum = jnp.sum(sums * factor, axis=0, keepdims=True) + own_weight * v_dec
    own_cols(ctx, rows, TILE)[...] = jnp.broadcast_to(dec_sum / dec_total, (TILE, cols)).astype(BF16)
    pending += tile_exchange(ctx, e_send, e_recv)

    y = pair + first[rows_of(t), :].astype(F32)
    for k in (1, 3, 2):
        send(
            to_chip.at[k - 1], from_chip.at[k - 1], b_send.at[k - 1], b_recv.at[k - 1], {"tensor": sib}
        ).wait_recv()
        y = y + from_chip[k - 1].astype(F32)
    result[...] = norm(y, gain2, shift2).astype(BF16)
    pre_out[rows_of(t), :] = result[:, pl.ds(pl.multiple_of(t * cols, cols), cols)]
    for d in range(1, n_tensor):
        to = lax.rem(t + d, n_tensor)
        copy = send(
            result.at[:, pl.ds(pl.multiple_of(to * cols, cols), cols)], pre_out.at[rows_of(t), :],
            o_send.at[d - 1], o_recv.at[d - 1], {"tensor": to},
        )
        copy.start()
        pending.append(copy)

    tile_arrival(ctx, e_send, e_recv)
    term = feed_forward(rows, TILE, TILE)[0:1, :].astype(BF16).astype(F32)
    dec_term[pl.ds(t, 1)] = term.reshape(1, 1, width)
    for d in range(1, n_tensor):
        copy = send(
            dec_term.at[t], dec_term.at[t], t_send.at[d - 1], t_recv.at[d - 1],
            {"tensor": lax.rem(t + d, n_tensor)},
        )
        copy.start()
        pending.append(copy)
    q_wait(q_all.at[pl.ds(0, n_req - 1)], q_send)
    q_wait(partial.at[pl.ds(0, n_req - 1)], p_send)
    for d in range(1, n_tensor):
        part = dec_term.at[lax.rem(t - d + n_tensor, n_tensor)]
        send(part, part, t_send.at[d - 1], t_recv.at[d - 1], {"tensor": sib}).wait_recv()
    dec_y = first[pl.ds(rows, TILE), :].astype(F32)[0:1, :] + jnp.sum(dec_term[:, 0, :], axis=0, keepdims=True)
    acc[pl.ds(rows, 8), :] = jnp.broadcast_to(norm(dec_y, gain2, shift2), (8, width))
    dec_out[...] = acc[pl.ds(rows, 8), pl.ds(pl.multiple_of(t * cols, cols), cols)][0:1, :].astype(BF16)

    for d in range(1, n_tensor):
        part = pre_out.at[rows_of(lax.rem(t - d + n_tensor, n_tensor)), :]
        send(part, part, o_send.at[d - 1], o_recv.at[d - 1], {"tensor": sib}).wait_recv()
    for copy in pending:
        copy.wait_send()


def local(
    pre_tokens, dec_tokens, req_of, page_table, page_place, cache_lengths, cache_keys, cache_values,
    w_qkv, w_out, ln1_gain, ln1_bias, w_up, w_down, ln2_gain, ln2_bias,
    *, n_req, n_tensor,
):
    rows, cols = pre_tokens.shape
    width = w_qkv.shape[0]
    hidden = w_up.shape[1]
    n_keys = cache_keys.shape[0] * cache_keys.shape[1]
    share = rows // n_tensor
    n_chip = n_tensor // 2
    args = (
        pre_tokens, dec_tokens, req_of, page_table.T, page_place, cache_lengths,
        cache_keys.reshape(n_keys, cols), cache_values.reshape(n_keys, cols),
        jnp.transpose(w_qkv, (1, 0, 2)), w_out, ln1_gain, ln1_bias, w_up, w_down, ln2_gain, ln2_bias,
    )
    sem = pltpu.SemaphoreType.DMA
    vm = pltpu.VMEM
    scratch = [
        vm((rows + TILE, width), BF16),
        vm((rows + TILE, width), BF16),
        vm((rows + TILE, width), BF16),
        vm((3, width, cols), BF16),
        vm((width, width), BF16),
        vm((width, hidden), BF16),
        vm((hidden, width), BF16),
        vm((n_keys, cols), BF16),
        vm((n_keys, cols), BF16),
        vm((1, cols), BF16),
        vm(req_of.shape, jnp.int32),
        vm(page_table.shape[::-1], jnp.int32),
        vm(page_place.shape, jnp.int32),
        vm(cache_lengths.shape, jnp.int32),
        vm((width,), F32), vm((width,), F32), vm((width,), F32), vm((width,), F32),
        vm((n_req, 1, cols), F32),
        vm((n_req, 2, cols), F32),
        vm((n_req, 2, cols), F32),
        vm((rows + TILE, width), F32),
        vm((rows, width), BF16),
        vm((n_chip, share, width), BF16),
        vm((n_chip - 1, share, width), BF16),
        vm((n_chip - 1, share, width), BF16),
        vm((share, width), BF16),
        vm((n_tensor, 1, width), F32),
        sem((7,)), sem((9,)),
        sem((9,)), sem((9,)), sem((7,)), sem((7,)), sem((9,)), sem((9,)), sem((7,)), sem((7,)),
        sem((9,)), sem((9,)),
        sem, sem, sem, sem,
        sem((4,)), sem((4,)), sem((3,)), sem((3,)), sem((7,)), sem((7,)), sem((7,)), sem((7,)),
    ]
    return pl.pallas_call(
        functools.partial(kernel, n_req=n_req, n_tensor=n_tensor),
        out_shape=(
            jax.ShapeDtypeStruct((rows, cols), BF16),
            jax.ShapeDtypeStruct((1, cols), BF16),
        ),
        in_specs=[pl.BlockSpec(memory_space=pltpu.HBM)] * len(args),
        out_specs=(
            pl.BlockSpec(memory_space=pltpu.VMEM),
            pl.BlockSpec(memory_space=pltpu.VMEM),
        ),
        scratch_shapes=scratch,
        compiler_params=pltpu.CompilerParams(
            collective_id=0, has_side_effects=True, vmem_limit_bytes=56 << 20
        ),
        name="layer",
    )(*args)


def solution(mesh):
    in_specs = (
        P("req", "tensor"),
        P("req", "tensor"),
        P(),
        P(),
        P(),
        P(),
        P("req", None, "tensor"),
        P("req", None, "tensor"),
        P(None, None, "tensor"),
        P("tensor", None),
        P(),
        P(),
        P(None, "tensor"),
        P("tensor", None),
        P(),
        P(),
    )
    out_specs = (P("req", "tensor"), P("req", "tensor"))
    body = functools.partial(local, n_req=mesh.shape["req"], n_tensor=mesh.shape["tensor"])
    return jax.shard_map(body, mesh=mesh, in_specs=in_specs, out_specs=out_specs, check_vma=False)
```

```python
import functools
import math

import jax
import jax.numpy as jnp
from jax import lax
from jax.experimental import pallas as pl
from jax.experimental.pallas import tpu as pltpu
from jax.sharding import PartitionSpec as P

MESH = pl.DeviceIdType.MESH
HD = 64
EPS = 1e-05
NEG = -1e30
F32 = jnp.float32
BF16 = jnp.bfloat16
TILE = 16


def dot(a, b, ca=1, cb=0):
    return lax.dot_general(a, b, (((ca,), (cb,)), ((), ())), preferred_element_type=F32)


def norm(total, gain, shift):
    mean = jnp.mean(total, axis=-1, keepdims=True)
    centered = total - mean
    var = jnp.mean(centered * centered, axis=-1, keepdims=True)
    return centered * lax.rsqrt(var + EPS) * gain + shift


def iota(shape, dim):
    return lax.broadcasted_iota(jnp.int32, shape, dim)


def kernel(
    pre_hbm, dec_hbm, req_hbm, table_hbm, place_hbm, len_hbm, keys_hbm, values_hbm,
    wqkv_hbm, wout_hbm, g1_hbm, b1_hbm, wup_hbm, wdown_hbm, g2_hbm, b2_hbm,
    pre_out, dec_out,
    x, ctx, first, wqkv, wout, wup, wdown, keys, values,
    dec_in, req, table, place, lens, g1, b1, g2, b2,
    q_all, partial, partial_all, acc, stage, from_pair, to_chip, from_chip, result, dec_term,
    local_sem, small_sem,
    x_send, x_recv, d_send, d_recv, c_send, c_recv, e_send, e_recv, w_send, w_recv,
    q_send, q_recv, p_send, p_recv, a_send, a_recv, b_send, b_recv, t_send, t_recv, o_send, o_recv,
    *, n_req, n_tensor,
):
    rows = pre_hbm.shape[0]
    cols = pre_hbm.shape[1]
    width = cols * n_tensor
    pages = keys_hbm.shape[0] // 128
    n_chip = n_tensor // 2
    share = rows // n_tensor
    me = lax.axis_index("req")
    t = lax.axis_index("tensor")
    chip = t // 2
    core = lax.rem(t, 2)
    sib = t + 1 - 2 * core

    def on_chip(k, c):
        return lax.rem(chip + k, n_chip) * 2 + c

    def send(src, dst, ss, rs, dev):
        return pltpu.make_async_remote_copy(
            src_ref=src, dst_ref=dst, send_sem=ss, recv_sem=rs, device_id=dev, device_id_type=MESH
        )

    n_z = 16 if n_req % 16 == 0 else n_req
    n_y = n_req // n_z
    ys = sorted(range(n_y), key=lambda dy: -min(dy, n_y - dy))

    def each_peer(visit):
        my, mz = me // n_z, lax.rem(me, n_z)

        def visit_ring(dz, dys):
            for dy in dys:
                visit(lax.rem(my + dy, n_y) * n_z + lax.rem(mz + dz, n_z))

        def both_ways(i, carry):
            dz = n_z // 2 - 1 - i
            visit_ring(dz, ys)
            visit_ring(n_z - dz, ys)
            return carry

        visit_ring(n_z // 2, ys)
        lax.fori_loop(0, n_z // 2 - 1, both_ways, 0)
        visit_ring(0, [dy for dy in ys if dy])

    barrier = pltpu.get_barrier_semaphore()
    for d in range(1, n_tensor):
        pl.semaphore_signal(
            barrier, inc=1, device_id={"tensor": lax.rem(t + d, n_tensor)}, device_id_type=MESH
        )
    each_peer(
        lambda to: pl.semaphore_signal(barrier, inc=1, device_id={"req": to}, device_id_type=MESH)
    )

    loads = [
        (dec_hbm, dec_in), (place_hbm, place), (table_hbm, table), (req_hbm, req), (len_hbm, lens),
        (g1_hbm, g1), (b1_hbm, b1), (g2_hbm, g2), (b2_hbm, b2),
    ]
    small = [pltpu.make_async_copy(a, b, small_sem.at[i]) for i, (a, b) in enumerate(loads)]
    small[0].start()

    def start_loads():
        for copy in big + small[1:]:
            copy.start()

    def own_cols(ref, lo, n):
        return ref.at[pl.ds(lo, n), pl.ds(pl.multiple_of(t * cols, cols), cols)]

    def cols_of(ref, lo, n, who):
        return ref.at[pl.ds(lo, n), pl.ds(pl.multiple_of(who * cols, cols), cols)]

    big = [
        pltpu.make_async_copy(wqkv_hbm, wqkv, local_sem.at[0]),
        pltpu.make_async_copy(pre_hbm, own_cols(x, 0, rows), local_sem.at[1]),
        pltpu.make_async_copy(keys_hbm, keys, local_sem.at[2]),
        pltpu.make_async_copy(values_hbm, values, local_sem.at[3]),
        pltpu.make_async_copy(
            wout_hbm, wout.at[pl.ds(pl.multiple_of(t * cols, cols), cols), :], local_sem.at[4]
        ),
        pltpu.make_async_copy(wup_hbm, wup, local_sem.at[5]),
        pltpu.make_async_copy(wdown_hbm, wdown, local_sem.at[6]),
    ]

    pending = []
    small[0].wait()
    tile = jnp.broadcast_to(dec_in[...].astype(F32), (TILE, cols)).astype(BF16)
    own_cols(x, rows, TILE)[...] = tile

    pl.semaphore_wait(barrier, n_tensor - 1 + n_req - 1)

    def tile_exchange(ref, ss, rs):
        out = []
        for d in sorted(range(1, n_tensor), key=lambda d: abs(d - n_tensor // 2)):
            copy = send(
                own_cols(ref, rows, TILE), own_cols(ref, rows, TILE), ss.at[d - 1], rs.at[d - 1],
                {"tensor": lax.rem(t + d, n_tensor)},
            )
            copy.start()
            out.append(copy)
        return out

    def tile_arrival(ref, ss, rs):
        for d in range(1, n_tensor):
            part = cols_of(ref, rows, TILE, lax.rem(t - d + n_tensor, n_tensor))
            send(part, part, ss.at[d - 1], rs.at[d - 1], {"tensor": sib}).wait_recv()

    def gather(own, region, ss, rs):
        def go(i, src, dst, dev):
            copy = send(src, dst, ss.at[i], rs.at[i], {"tensor": dev})
            copy.start()
            pending.append(copy)

        def arrived(i, ref):
            send(ref, ref, ss.at[i], rs.at[i], {"tensor": sib}).wait_recv()

        def begin():
            for k in (2, 1, 3):
                go(k, own, region(t), on_chip(k, core))
            go(0, own, region(t), sib)

        def forward(*ks):
            for k in ks:
                part = region(on_chip(n_chip - k, core))
                arrived(k, part)
                go(3 + k, part, part, sib)

        def end():
            arrived(0, region(sib))
            for k in (1, 3, 2):
                arrived(3 + k, region(on_chip(n_chip - k, 1 - core)))

        return begin, forward, end

    right, left, far = on_chip(1, core), on_chip(n_chip - 1, core), on_chip(2, core)

    def relay(own, region, ss, rs):
        def split(ref):
            n = ref.shape[0] // 2
            return ref.at[pl.ds(0, n), :], ref.at[pl.ds(n, n), :]

        def go(i, src, dst, dev):
            copy = send(src, dst, ss.at[i], rs.at[i], {"tensor": dev})
            copy.start()
            pending.append(copy)

        def arrived(i, ref):
            send(ref, ref, ss.at[i], rs.at[i], {"tensor": sib}).wait_recv()

        def begin():
            (own_top, own_bottom), (top, bottom) = split(own), split(region(t))
            go(1, own_top, top, right)
            go(2, own_bottom, bottom, left)
            go(3, own_bottom, bottom, right)
            go(4, own_top, top, left)
            go(0, own, region(t), sib)

        def onward():
            top, _ = split(region(left))
            arrived(1, top)
            go(5, top, top, right)
            _, bottom = split(region(right))
            arrived(2, bottom)
            go(6, bottom, bottom, left)

        def near():
            _, bottom = split(region(left))
            arrived(3, bottom)
            go(7, region(left), region(left), sib)
            top, _ = split(region(right))
            arrived(4, top)
            go(8, region(right), region(right), sib)

        def across():
            top, bottom = split(region(far))
            arrived(5, top)
            arrived(6, bottom)
            go(9, region(far), region(far), sib)

        def end():
            arrived(0, region(sib))
            arrived(7, region(on_chip(n_chip - 1, 1 - core)))
            arrived(8, region(on_chip(1, 1 - core)))
            arrived(9, region(on_chip(2, 1 - core)))

        return begin, onward, near, across, end

    def x_region(who):
        return cols_of(x, 0, rows, who)

    def c_region(who):
        return cols_of(ctx, 0, rows, who)

    def w_region(who):
        return wout.at[pl.ds(pl.multiple_of(who * cols, cols), cols), :]

    gather_x = gather(pre_hbm, x_region, x_send, x_recv)
    gather_w = relay(wout_hbm, w_region, w_send, w_recv)
    gather_c = gather(own_cols(ctx, 0, rows), c_region, c_send, c_recv)

    pending += tile_exchange(x, d_send, d_recv)
    gather_x[0]()
    start_loads()
    gather_w[0]()

    lane = iota((1, cols), 1)
    low_head = lane < HD
    big[0].wait()
    tile_arrival(x, d_send, d_recv)
    x_dec = x[pl.ds(rows, TILE), :]
    q_dec = dot(x_dec, wqkv[0]).astype(BF16).astype(F32)[0:1, :]
    q_all[pl.ds(me, 1)] = q_dec.reshape(1, 1, cols)
    each_peer(lambda to: send(q_all.at[me], q_all.at[me], q_send, q_recv, {"req": to}).start())
    k_dec = dot(x_dec, wqkv[1]).astype(BF16).astype(F32)[0:1, :]
    v_dec = dot(x_dec, wqkv[2]).astype(BF16).astype(F32)[0:1, :]

    gather_x[1](1, 3, 2)
    for copy in small[1:]:
        copy.wait()
    n_page_ids = place.shape[0]
    n_r = req.shape[0]
    place_row = place[...].reshape(1, n_page_ids)
    held = place_row == (iota((TILE, n_page_ids), 0) + me * pages)
    page_id = jnp.sum(
        jnp.where(held, iota((TILE, n_page_ids), 1).astype(F32), 0.0), axis=1, keepdims=True
    )
    ids = table[...].astype(F32)
    in_page = jnp.clip(
        lens[...].reshape(1, n_r) - 128 * iota(table.shape, 0), 0, 128
    ).astype(F32)
    sub = iota((TILE, n_r), 0)
    tokens = jnp.zeros((TILE, n_r), F32)
    for s in range(pages):
        hit = jnp.sum(
            jnp.where(ids == page_id[s : s + 1, 0:1], in_page, 0.0), axis=0, keepdims=True
        )
        tokens = tokens + jnp.where(sub == s, hit, 0.0)
    req_row = jnp.broadcast_to(req[...].reshape(1, n_r).astype(F32), (8, n_r))
    lane_slot = lax.rem(iota((n_r, 2 * n_r), 1), n_r)
    twice = (iota((n_r, 2 * n_r), 0) == lane_slot).astype(F32).astype(BF16)
    req_twice = dot(req_row.astype(BF16), twice)[0:1, :]
    pick = (iota((n_r, 2 * n_r), 0).astype(F32) == req_twice).astype(F32).astype(BF16)
    in_slot = dot(tokens.astype(BF16), pick)

    gather_w[1]()
    gather_x[2]()
    big[1].wait()
    x_pre = x[pl.ds(0, rows), :]
    q = dot(x_pre, wqkv[0])
    k = dot(x_pre, wqkv[1]).astype(BF16)
    v = dot(x_pre, wqkv[2]).astype(BF16)
    scale = 1.0 / math.sqrt(HD)
    causal = iota((rows, rows), 0) >= iota((rows, rows), 1)
    heads = []
    for h in range(2):
        qh = jnp.where(low_head if h == 0 else ~low_head, q, 0.0).astype(BF16)
        scores = jnp.where(causal, dot(qh, k, 1, 1) * scale, NEG)
        top = jnp.max(scores, axis=-1, keepdims=True)
        weights = jnp.where(causal, jnp.exp(scores - top), 0.0)
        total = jnp.sum(weights, axis=-1, keepdims=True)
        heads.append(dot(weights.astype(BF16), v) / total)
    own_cols(ctx, 0, rows)[...] = jnp.where(low_head, heads[0], heads[1]).astype(BF16)
    gather_c[0]()

    def q_wait(ref, sem):
        pltpu.make_async_copy(ref, ref, sem).wait()

    big[2].wait()
    big[3].wait()
    q_wait(q_all.at[pl.ds(0, n_req - 1)], q_recv)
    q_slots = q_all[:, 0, :]
    both = jnp.concatenate(
        [jnp.where(low_head, q_slots, 0.0), jnp.where(low_head, 0.0, q_slots)], axis=0
    ).astype(BF16)
    scores = dot(keys[...], both, 1, 1) * scale
    row_in_page = iota((128, 2 * n_req), 0).astype(F32)
    masks = [row_in_page < in_slot[s : s + 1, :] for s in range(pages)]
    parts = [
        jnp.where(masks[s], scores[s * 128 : (s + 1) * 128], NEG) for s in range(pages)
    ]
    top = functools.reduce(jnp.maximum, parts)
    top = jnp.max(top, axis=0, keepdims=True)
    parts = [jnp.where(m, jnp.exp(p - top), 0.0) for m, p in zip(masks, parts)]
    total = jnp.sum(functools.reduce(jnp.add, parts), axis=0, keepdims=True)
    weights = jnp.concatenate(parts, axis=0).astype(BF16)
    summed = dot(weights, values[...], 0, 0)
    diag = iota((2 * n_req, 2 * n_req), 0) == iota((2 * n_req, 2 * n_req), 1)

    def per_slot(row):
        column = jnp.sum(jnp.where(diag, row, 0.0), axis=1, keepdims=True)
        return jnp.where(low_head, column[:n_req], column[n_req:])

    first_half = lax.rem(lane, HD) < HD // 2
    partial[:, 0, :] = jnp.where(low_head, summed[:n_req], summed[n_req:])
    partial[:, 1, :] = jnp.where(first_half, per_slot(top), per_slot(total))
    partial_all[pl.ds(me, 1)] = partial[pl.ds(me, 1)]
    each_peer(lambda to: send(partial.at[to], partial_all.at[me], p_send, p_recv, {"req": to}).start())

    gather_w[2]()
    gather_c[1](1, 3, 2)
    gather_w[3]()
    gain1 = g1[...].reshape(1, width)
    shift1 = b1[...].reshape(1, width)
    gain2 = g2[...].reshape(1, width)
    shift2 = b2[...].reshape(1, width)

    def feed_forward(lo, n, chunk):
        acc[pl.ds(lo, n), :] = dot(ctx[pl.ds(lo, n), :], wout[...])
        for at in range(lo, lo + n, chunk):
            total = x[pl.ds(at, chunk), :].astype(F32) + acc[pl.ds(at, chunk), :]
            first[pl.ds(at, chunk), :] = norm(total, gain1, shift1).astype(BF16)
        up = dot(first[pl.ds(lo, n), :], wup[...])
        hidden = (0.5 * up * (1.0 + lax.erf(up * (1.0 / math.sqrt(2.0))))).astype(BF16)
        return dot(hidden, wdown[...])

    def dec_merge():
        q_wait(partial_all.at[pl.ds(0, n_req - 1)], p_recv)
        sums = partial_all[:, 0, :]
        stats = partial_all[:, 1, :]
        tops = jnp.where(first_half, stats, pltpu.roll(stats, HD // 2, 1))
        totals = jnp.where(first_half, pltpu.roll(stats, cols - HD // 2, 1), stats)
        qk = q_dec * k_dec
        own_score = scale * jnp.where(
            low_head,
            jnp.sum(jnp.where(low_head, qk, 0.0), axis=1, keepdims=True),
            jnp.sum(jnp.where(low_head, 0.0, qk), axis=1, keepdims=True),
        )
        best = jnp.maximum(jnp.max(tops, axis=0, keepdims=True), own_score)
        factor = jnp.exp(tops - best)
        own_weight = jnp.exp(own_score - best)
        dec_total = jnp.sum(totals * factor, axis=0, keepdims=True) + own_weight
        dec_sum = jnp.sum(sums * factor, axis=0, keepdims=True) + own_weight * v_dec
        own_cols(ctx, rows, TILE)[...] = jnp.broadcast_to(dec_sum / dec_total, (TILE, cols)).astype(BF16)
        pending.extend(tile_exchange(ctx, e_send, e_recv))

    last = []

    def dec_tail():
        tile_arrival(ctx, e_send, e_recv)
        term = feed_forward(rows, TILE, TILE)[0:1, :].astype(BF16).astype(F32)
        dec_term[pl.ds(t, 1)] = term.reshape(1, 1, width)
        for d in range(1, n_tensor):
            copy = send(
                dec_term.at[t], dec_term.at[t], t_send.at[d - 1], t_recv.at[d - 1],
                {"tensor": lax.rem(t + d, n_tensor)},
            )
            copy.start()
            last.append(copy)

    def drain():
        q_wait(q_all.at[pl.ds(0, n_req - 1)], q_send)
        q_wait(partial.at[pl.ds(0, n_req - 1)], p_send)
        for copy in pending:
            copy.wait_send()

    big[4].wait()
    big[5].wait()
    big[6].wait()
    gather_c[2]()
    gather_w[4]()
    stage[...] = feed_forward(0, rows, 64).astype(BF16)

    def rows_of(who):
        return pl.ds(pl.multiple_of(who * share, share), share)

    for k in range(n_chip):
        to = on_chip(k, 1 - core)
        copy = send(stage.at[rows_of(to), :], from_pair.at[k], a_send.at[k], a_recv.at[k], {"tensor": sib})
        copy.start()
        pending.append(copy)
    dec_merge()
    for k in (2, 1, 3, 0):
        to = on_chip(k, core)
        send(stage.at[rows_of(to), :], from_pair.at[k], a_send.at[k], a_recv.at[k], {"tensor": sib}).wait_recv()
        pair = stage[rows_of(to), :].astype(F32) + from_pair[k].astype(F32)
        if k:
            to_chip[k - 1] = pair.astype(BF16)
            copy = send(
                to_chip.at[k - 1], from_chip.at[k - 1], b_send.at[k - 1], b_recv.at[k - 1], {"tensor": to}
            )
            copy.start()
            pending.append(copy)

    dec_tail()

    y = pair + first[rows_of(t), :].astype(F32)
    for k in (1, 3, 2):
        send(
            to_chip.at[k - 1], from_chip.at[k - 1], b_send.at[k - 1], b_recv.at[k - 1], {"tensor": sib}
        ).wait_recv()
        y = y + from_chip[k - 1].astype(F32)
    result[...] = norm(y, gain2, shift2).astype(BF16)
    pre_out[rows_of(t), :] = result[:, pl.ds(pl.multiple_of(t * cols, cols), cols)]
    for d in range(1, n_tensor):
        to = lax.rem(t + d, n_tensor)
        copy = send(
            result.at[:, pl.ds(pl.multiple_of(to * cols, cols), cols)], pre_out.at[rows_of(t), :],
            o_send.at[d - 1], o_recv.at[d - 1], {"tensor": to},
        )
        copy.start()
        pending.append(copy)

    drain()

    for d in range(1, n_tensor):
        part = dec_term.at[lax.rem(t - d + n_tensor, n_tensor)]
        send(part, part, t_send.at[d - 1], t_recv.at[d - 1], {"tensor": sib}).wait_recv()
    dec_y = first[pl.ds(rows, TILE), :].astype(F32)[0:1, :] + jnp.sum(dec_term[:, 0, :], axis=0, keepdims=True)
    acc[pl.ds(rows, 8), :] = jnp.broadcast_to(norm(dec_y, gain2, shift2), (8, width))
    dec_out[...] = acc[pl.ds(rows, 8), pl.ds(pl.multiple_of(t * cols, cols), cols)][0:1, :].astype(BF16)

    for d in range(1, n_tensor):
        part = pre_out.at[rows_of(lax.rem(t - d + n_tensor, n_tensor)), :]
        send(part, part, o_send.at[d - 1], o_recv.at[d - 1], {"tensor": sib}).wait_recv()
    for copy in last:
        copy.wait_send()


def local(
    pre_tokens, dec_tokens, req_of, page_table, page_place, cache_lengths, cache_keys, cache_values,
    w_qkv, w_out, ln1_gain, ln1_bias, w_up, w_down, ln2_gain, ln2_bias,
    *, n_req, n_tensor,
):
    rows, cols = pre_tokens.shape
    width = w_qkv.shape[0]
    hidden = w_up.shape[1]
    n_keys = cache_keys.shape[0] * cache_keys.shape[1]
    share = rows // n_tensor
    n_chip = n_tensor // 2
    args = (
        pre_tokens, dec_tokens, req_of, page_table.T, page_place, cache_lengths,
        cache_keys.reshape(n_keys, cols), cache_values.reshape(n_keys, cols),
        jnp.transpose(w_qkv, (1, 0, 2)), w_out, ln1_gain, ln1_bias, w_up, w_down, ln2_gain, ln2_bias,
    )
    sem = pltpu.SemaphoreType.DMA
    vm = pltpu.VMEM
    scratch = [
        vm((rows + TILE, width), BF16),
        vm((rows + TILE, width), BF16),
        vm((rows + TILE, width), BF16),
        vm((3, width, cols), BF16),
        vm((width, width), BF16),
        vm((width, hidden), BF16),
        vm((hidden, width), BF16),
        vm((n_keys, cols), BF16),
        vm((n_keys, cols), BF16),
        vm((1, cols), BF16),
        vm(req_of.shape, jnp.int32),
        vm(page_table.shape[::-1], jnp.int32),
        vm(page_place.shape, jnp.int32),
        vm(cache_lengths.shape, jnp.int32),
        vm((width,), F32), vm((width,), F32), vm((width,), F32), vm((width,), F32),
        vm((n_req, 1, cols), F32),
        vm((n_req, 2, cols), F32),
        vm((n_req, 2, cols), F32),
        vm((rows + TILE, width), F32),
        vm((rows, width), BF16),
        vm((n_chip, share, width), BF16),
        vm((n_chip - 1, share, width), BF16),
        vm((n_chip - 1, share, width), BF16),
        vm((share, width), BF16),
        vm((n_tensor, 1, width), F32),
        sem((7,)), sem((9,)),
        sem((9,)), sem((9,)), sem((7,)), sem((7,)), sem((9,)), sem((9,)), sem((7,)), sem((7,)),
        sem((10,)), sem((10,)),
        sem, sem, sem, sem,
        sem((4,)), sem((4,)), sem((3,)), sem((3,)), sem((7,)), sem((7,)), sem((7,)), sem((7,)),
    ]
    return pl.pallas_call(
        functools.partial(kernel, n_req=n_req, n_tensor=n_tensor),
        out_shape=(
            jax.ShapeDtypeStruct((rows, cols), BF16),
            jax.ShapeDtypeStruct((1, cols), BF16),
        ),
        in_specs=[pl.BlockSpec(memory_space=pltpu.HBM)] * len(args),
        out_specs=(
            pl.BlockSpec(memory_space=pltpu.VMEM),
            pl.BlockSpec(memory_space=pltpu.VMEM),
        ),
        scratch_shapes=scratch,
        compiler_params=pltpu.CompilerParams(
            collective_id=0, has_side_effects=True, vmem_limit_bytes=56 << 20
        ),
        name="layer",
    )(*args)


def solution(mesh):
    in_specs = (
        P("req", "tensor"),
        P("req", "tensor"),
        P(),
        P(),
        P(),
        P(),
        P("req", None, "tensor"),
        P("req", None, "tensor"),
        P(None, None, "tensor"),
        P("tensor", None),
        P(),
        P(),
        P(None, "tensor"),
        P("tensor", None),
        P(),
        P(),
    )
    out_specs = (P("req", "tensor"), P("req", "tensor"))
    body = functools.partial(local, n_req=mesh.shape["req"], n_tensor=mesh.shape["tensor"])
    return jax.shard_map(body, mesh=mesh, in_specs=in_specs, out_specs=out_specs, check_vma=False)
```

```python
import functools
import math

import jax
import jax.numpy as jnp
from jax import lax
from jax.experimental import pallas as pl
from jax.experimental.pallas import tpu as pltpu
from jax.sharding import PartitionSpec as P

MESH = pl.DeviceIdType.MESH
HD = 64
EPS = 1e-05
NEG = -1e30
F32 = jnp.float32
BF16 = jnp.bfloat16
TILE = 16


def dot(a, b, ca=1, cb=0):
    return lax.dot_general(a, b, (((ca,), (cb,)), ((), ())), preferred_element_type=F32)


def norm(total, gain, shift):
    mean = jnp.mean(total, axis=-1, keepdims=True)
    centered = total - mean
    var = jnp.mean(centered * centered, axis=-1, keepdims=True)
    return centered * lax.rsqrt(var + EPS) * gain + shift


def iota(shape, dim):
    return lax.broadcasted_iota(jnp.int32, shape, dim)


def kernel(
    pre_hbm, dec_hbm, req_hbm, table_hbm, place_hbm, len_hbm, keys_hbm, values_hbm,
    wqkv_hbm, wout_hbm, g1_hbm, b1_hbm, wup_hbm, wdown_hbm, g2_hbm, b2_hbm,
    pre_out, dec_out,
    x, ctx, first, wqkv, wout, wup, wdown, keys, values,
    dec_in, req, table, place, lens, g1, b1, g2, b2,
    q_all, partial, partial_all, acc, stage, from_pair, to_chip, from_chip, result, dec_term,
    local_sem, small_sem, ring_in,
    x_send, x_recv, d_send, d_recv, c_send, c_recv, e_send, e_recv, w_send, w_recv,
    q_send, q_recv, p_send, p_recv, a_send, a_recv, b_send, b_recv, t_send, t_recv, o_send, o_recv,
    *, n_req, n_tensor,
):
    rows = pre_hbm.shape[0]
    cols = pre_hbm.shape[1]
    width = cols * n_tensor
    pages = keys_hbm.shape[0] // 128
    n_chip = n_tensor // 2
    share = rows // n_tensor
    me = lax.axis_index("req")
    t = lax.axis_index("tensor")
    chip = t // 2
    core = lax.rem(t, 2)
    sib = t + 1 - 2 * core

    def on_chip(k, c):
        return lax.rem(chip + k, n_chip) * 2 + c

    def send(src, dst, ss, rs, dev):
        return pltpu.make_async_remote_copy(
            src_ref=src, dst_ref=dst, send_sem=ss, recv_sem=rs, device_id=dev, device_id_type=MESH
        )

    n_z = 16 if n_req % 16 == 0 else n_req
    n_y = n_req // n_z
    ys = sorted(range(n_y), key=lambda dy: -min(dy, n_y - dy))

    def each_peer(visit):
        my, mz = me // n_z, lax.rem(me, n_z)

        def visit_ring(dz, dys):
            for dy in dys:
                visit(lax.rem(my + dy, n_y) * n_z + lax.rem(mz + dz, n_z))

        def both_ways(i, carry):
            dz = n_z // 2 - 1 - i
            visit_ring(dz, ys)
            visit_ring(n_z - dz, ys)
            return carry

        visit_ring(n_z // 2, ys)
        lax.fori_loop(0, n_z // 2 - 1, both_ways, 0)
        visit_ring(0, [dy for dy in ys if dy])

    barrier = pltpu.get_barrier_semaphore()
    for d in range(1, n_tensor):
        pl.semaphore_signal(
            barrier, inc=1, device_id={"tensor": lax.rem(t + d, n_tensor)}, device_id_type=MESH
        )
    my, mz = me // n_z, lax.rem(me, n_z)
    columns = [lax.rem(my + dy, n_y) * n_z + mz for dy in ys if dy]
    ring = [
        my * n_z + lax.rem(mz + dz, n_z)
        for dz in sorted(range(1, n_z), key=lambda dz: -min(dz, n_z - dz))
    ]
    for to in ring + columns:
        pl.semaphore_signal(barrier, inc=1, device_id={"req": to}, device_id_type=MESH)

    loads = [
        (dec_hbm, dec_in), (place_hbm, place), (table_hbm, table), (req_hbm, req), (len_hbm, lens),
        (g1_hbm, g1), (b1_hbm, b1), (g2_hbm, g2), (b2_hbm, b2),
    ]
    small = [pltpu.make_async_copy(a, b, small_sem.at[i]) for i, (a, b) in enumerate(loads)]
    small[0].start()

    def start_loads():
        for copy in big + small[1:]:
            copy.start()

    def own_cols(ref, lo, n):
        return ref.at[pl.ds(lo, n), pl.ds(pl.multiple_of(t * cols, cols), cols)]

    def cols_of(ref, lo, n, who):
        return ref.at[pl.ds(lo, n), pl.ds(pl.multiple_of(who * cols, cols), cols)]

    big = [
        pltpu.make_async_copy(wqkv_hbm, wqkv, local_sem.at[0]),
        pltpu.make_async_copy(pre_hbm, own_cols(x, 0, rows), local_sem.at[1]),
        pltpu.make_async_copy(keys_hbm, keys, local_sem.at[2]),
        pltpu.make_async_copy(values_hbm, values, local_sem.at[3]),
        pltpu.make_async_copy(
            wout_hbm, wout.at[pl.ds(pl.multiple_of(t * cols, cols), cols), :], local_sem.at[4]
        ),
        pltpu.make_async_copy(wup_hbm, wup, local_sem.at[5]),
        pltpu.make_async_copy(wdown_hbm, wdown, local_sem.at[6]),
    ]

    pending = []
    small[0].wait()
    tile = jnp.broadcast_to(dec_in[...].astype(F32), (TILE, cols)).astype(BF16)
    own_cols(x, rows, TILE)[...] = tile

    pl.semaphore_wait(barrier, n_tensor - 1 + len(ring) + len(columns))
    for to in columns:
        pl.semaphore_signal(ring_in, inc=1, device_id={"req": to}, device_id_type=MESH)

    def tile_exchange(ref, ss, rs):
        out = []
        for d in sorted(range(1, n_tensor), key=lambda d: abs(d - n_tensor // 2)):
            copy = send(
                own_cols(ref, rows, TILE), own_cols(ref, rows, TILE), ss.at[d - 1], rs.at[d - 1],
                {"tensor": lax.rem(t + d, n_tensor)},
            )
            copy.start()
            out.append(copy)
        return out

    def tile_arrival(ref, ss, rs):
        for d in range(1, n_tensor):
            part = cols_of(ref, rows, TILE, lax.rem(t - d + n_tensor, n_tensor))
            send(part, part, ss.at[d - 1], rs.at[d - 1], {"tensor": sib}).wait_recv()

    def gather(own, region, ss, rs):
        def go(i, src, dst, dev):
            copy = send(src, dst, ss.at[i], rs.at[i], {"tensor": dev})
            copy.start()
            pending.append(copy)

        def arrived(i, ref):
            send(ref, ref, ss.at[i], rs.at[i], {"tensor": sib}).wait_recv()

        def begin():
            for k in (2, 1, 3):
                go(k, own, region(t), on_chip(k, core))
            go(0, own, region(t), sib)

        def forward(*ks):
            for k in ks:
                part = region(on_chip(n_chip - k, core))
                arrived(k, part)
                go(3 + k, part, part, sib)

        def end():
            arrived(0, region(sib))
            for k in (1, 3, 2):
                arrived(3 + k, region(on_chip(n_chip - k, 1 - core)))

        return begin, forward, end

    right, left, far = on_chip(1, core), on_chip(n_chip - 1, core), on_chip(2, core)

    def relay(own, region, ss, rs):
        def split(ref):
            n = ref.shape[0] // 2
            return ref.at[pl.ds(0, n), :], ref.at[pl.ds(n, n), :]

        def go(i, src, dst, dev):
            copy = send(src, dst, ss.at[i], rs.at[i], {"tensor": dev})
            copy.start()
            pending.append(copy)

        def arrived(i, ref):
            send(ref, ref, ss.at[i], rs.at[i], {"tensor": sib}).wait_recv()

        def begin():
            (own_top, own_bottom), (top, bottom) = split(own), split(region(t))
            go(1, own_top, top, right)
            go(2, own_bottom, bottom, left)
            go(3, own_bottom, bottom, right)
            go(4, own_top, top, left)
            go(0, own, region(t), sib)

        def onward():
            top, _ = split(region(left))
            arrived(1, top)
            go(5, top, top, right)
            _, bottom = split(region(right))
            arrived(2, bottom)
            go(6, bottom, bottom, left)

        def near():
            _, bottom = split(region(left))
            arrived(3, bottom)
            go(7, region(left), region(left), sib)
            top, _ = split(region(right))
            arrived(4, top)
            go(8, region(right), region(right), sib)

        def across():
            top, bottom = split(region(far))
            arrived(5, top)
            arrived(6, bottom)
            go(9, region(far), region(far), sib)

        def end():
            arrived(0, region(sib))
            arrived(7, region(on_chip(n_chip - 1, 1 - core)))
            arrived(8, region(on_chip(1, 1 - core)))
            arrived(9, region(on_chip(2, 1 - core)))

        return begin, onward, near, across, end

    def x_region(who):
        return cols_of(x, 0, rows, who)

    def c_region(who):
        return cols_of(ctx, 0, rows, who)

    def w_region(who):
        return wout.at[pl.ds(pl.multiple_of(who * cols, cols), cols), :]

    gather_x = gather(pre_hbm, x_region, x_send, x_recv)
    gather_w = relay(wout_hbm, w_region, w_send, w_recv)
    gather_c = gather(own_cols(ctx, 0, rows), c_region, c_send, c_recv)

    pending += tile_exchange(x, d_send, d_recv)
    gather_x[0]()
    start_loads()
    gather_w[0]()

    lane = iota((1, cols), 1)
    low_head = lane < HD
    big[0].wait()
    tile_arrival(x, d_send, d_recv)
    x_dec = x[pl.ds(rows, TILE), :]
    q_dec = dot(x_dec, wqkv[0]).astype(BF16).astype(F32)[0:1, :]
    q_all[pl.ds(me, 1)] = q_dec.reshape(1, 1, cols)
    pl.semaphore_wait(ring_in, len(columns))
    each_peer(lambda to: send(q_all.at[me], q_all.at[me], q_send, q_recv, {"req": to}).start())
    k_dec = dot(x_dec, wqkv[1]).astype(BF16).astype(F32)[0:1, :]
    v_dec = dot(x_dec, wqkv[2]).astype(BF16).astype(F32)[0:1, :]

    gather_x[1](1, 3, 2)
    for copy in small[1:]:
        copy.wait()
    n_page_ids = place.shape[0]
    n_r = req.shape[0]
    place_row = place[...].reshape(1, n_page_ids)
    held = place_row == (iota((TILE, n_page_ids), 0) + me * pages)
    page_id = jnp.sum(
        jnp.where(held, iota((TILE, n_page_ids), 1).astype(F32), 0.0), axis=1, keepdims=True
    )
    ids = table[...].astype(F32)
    in_page = jnp.clip(
        lens[...].reshape(1, n_r) - 128 * iota(table.shape, 0), 0, 128
    ).astype(F32)
    sub = iota((TILE, n_r), 0)
    tokens = jnp.zeros((TILE, n_r), F32)
    for s in range(pages):
        hit = jnp.sum(
            jnp.where(ids == page_id[s : s + 1, 0:1], in_page, 0.0), axis=0, keepdims=True
        )
        tokens = tokens + jnp.where(sub == s, hit, 0.0)
    req_row = jnp.broadcast_to(req[...].reshape(1, n_r).astype(F32), (8, n_r))
    lane_slot = lax.rem(iota((n_r, 2 * n_r), 1), n_r)
    twice = (iota((n_r, 2 * n_r), 0) == lane_slot).astype(F32).astype(BF16)
    req_twice = dot(req_row.astype(BF16), twice)[0:1, :]
    pick = (iota((n_r, 2 * n_r), 0).astype(F32) == req_twice).astype(F32).astype(BF16)
    in_slot = dot(tokens.astype(BF16), pick)

    gather_w[1]()
    gather_x[2]()
    big[1].wait()
    x_pre = x[pl.ds(0, rows), :]
    q = dot(x_pre, wqkv[0])
    k = dot(x_pre, wqkv[1]).astype(BF16)
    v = dot(x_pre, wqkv[2]).astype(BF16)
    scale = 1.0 / math.sqrt(HD)
    causal = iota((rows, rows), 0) >= iota((rows, rows), 1)
    heads = []
    for h in range(2):
        qh = jnp.where(low_head if h == 0 else ~low_head, q, 0.0).astype(BF16)
        scores = jnp.where(causal, dot(qh, k, 1, 1) * scale, NEG)
        top = jnp.max(scores, axis=-1, keepdims=True)
        weights = jnp.where(causal, jnp.exp(scores - top), 0.0)
        total = jnp.sum(weights, axis=-1, keepdims=True)
        heads.append(dot(weights.astype(BF16), v) / total)
    own_cols(ctx, 0, rows)[...] = jnp.where(low_head, heads[0], heads[1]).astype(BF16)
    gather_c[0]()

    def q_wait(ref, sem):
        pltpu.make_async_copy(ref, ref, sem).wait()

    big[2].wait()
    big[3].wait()
    q_wait(q_all.at[pl.ds(0, n_req - 1)], q_recv)
    q_slots = q_all[:, 0, :]
    both = jnp.concatenate(
        [jnp.where(low_head, q_slots, 0.0), jnp.where(low_head, 0.0, q_slots)], axis=0
    ).astype(BF16)
    scores = dot(keys[...], both, 1, 1) * scale
    row_in_page = iota((128, 2 * n_req), 0).astype(F32)
    masks = [row_in_page < in_slot[s : s + 1, :] for s in range(pages)]
    parts = [
        jnp.where(masks[s], scores[s * 128 : (s + 1) * 128], NEG) for s in range(pages)
    ]
    top = functools.reduce(jnp.maximum, parts)
    top = jnp.max(top, axis=0, keepdims=True)
    parts = [jnp.where(m, jnp.exp(p - top), 0.0) for m, p in zip(masks, parts)]
    total = jnp.sum(functools.reduce(jnp.add, parts), axis=0, keepdims=True)
    weights = jnp.concatenate(parts, axis=0).astype(BF16)
    summed = dot(weights, values[...], 0, 0)
    diag = iota((2 * n_req, 2 * n_req), 0) == iota((2 * n_req, 2 * n_req), 1)

    def per_slot(row):
        column = jnp.sum(jnp.where(diag, row, 0.0), axis=1, keepdims=True)
        return jnp.where(low_head, column[:n_req], column[n_req:])

    first_half = lax.rem(lane, HD) < HD // 2
    partial[:, 0, :] = jnp.where(low_head, summed[:n_req], summed[n_req:])
    partial[:, 1, :] = jnp.where(first_half, per_slot(top), per_slot(total))
    partial_all[pl.ds(me, 1)] = partial[pl.ds(me, 1)]
    each_peer(lambda to: send(partial.at[to], partial_all.at[me], p_send, p_recv, {"req": to}).start())

    gather_w[2]()
    gather_c[1](1, 3, 2)
    gather_w[3]()
    gain1 = g1[...].reshape(1, width)
    shift1 = b1[...].reshape(1, width)
    gain2 = g2[...].reshape(1, width)
    shift2 = b2[...].reshape(1, width)

    def feed_forward(lo, n, chunk):
        acc[pl.ds(lo, n), :] = dot(ctx[pl.ds(lo, n), :], wout[...])
        for at in range(lo, lo + n, chunk):
            total = x[pl.ds(at, chunk), :].astype(F32) + acc[pl.ds(at, chunk), :]
            first[pl.ds(at, chunk), :] = norm(total, gain1, shift1).astype(BF16)
        up = dot(first[pl.ds(lo, n), :], wup[...])
        hidden = (0.5 * up * (1.0 + lax.erf(up * (1.0 / math.sqrt(2.0))))).astype(BF16)
        return dot(hidden, wdown[...])

    def dec_merge():
        q_wait(partial_all.at[pl.ds(0, n_req - 1)], p_recv)
        sums = partial_all[:, 0, :]
        stats = partial_all[:, 1, :]
        tops = jnp.where(first_half, stats, pltpu.roll(stats, HD // 2, 1))
        totals = jnp.where(first_half, pltpu.roll(stats, cols - HD // 2, 1), stats)
        qk = q_dec * k_dec
        own_score = scale * jnp.where(
            low_head,
            jnp.sum(jnp.where(low_head, qk, 0.0), axis=1, keepdims=True),
            jnp.sum(jnp.where(low_head, 0.0, qk), axis=1, keepdims=True),
        )
        best = jnp.maximum(jnp.max(tops, axis=0, keepdims=True), own_score)
        factor = jnp.exp(tops - best)
        own_weight = jnp.exp(own_score - best)
        dec_total = jnp.sum(totals * factor, axis=0, keepdims=True) + own_weight
        dec_sum = jnp.sum(sums * factor, axis=0, keepdims=True) + own_weight * v_dec
        own_cols(ctx, rows, TILE)[...] = jnp.broadcast_to(dec_sum / dec_total, (TILE, cols)).astype(BF16)
        pending.extend(tile_exchange(ctx, e_send, e_recv))

    last = []

    def dec_tail():
        tile_arrival(ctx, e_send, e_recv)
        term = feed_forward(rows, TILE, TILE)[0:1, :].astype(BF16).astype(F32)
        dec_term[pl.ds(t, 1)] = term.reshape(1, 1, width)
        for d in range(1, n_tensor):
            copy = send(
                dec_term.at[t], dec_term.at[t], t_send.at[d - 1], t_recv.at[d - 1],
                {"tensor": lax.rem(t + d, n_tensor)},
            )
            copy.start()
            last.append(copy)

    def drain():
        q_wait(q_all.at[pl.ds(0, n_req - 1)], q_send)
        q_wait(partial.at[pl.ds(0, n_req - 1)], p_send)
        for copy in pending:
            copy.wait_send()

    big[4].wait()
    big[5].wait()
    big[6].wait()
    gather_c[2]()
    gather_w[4]()
    stage[...] = feed_forward(0, rows, 64).astype(BF16)

    def rows_of(who):
        return pl.ds(pl.multiple_of(who * share, share), share)

    for k in range(n_chip):
        to = on_chip(k, 1 - core)
        copy = send(stage.at[rows_of(to), :], from_pair.at[k], a_send.at[k], a_recv.at[k], {"tensor": sib})
        copy.start()
        pending.append(copy)
    dec_merge()
    for k in (2, 1, 3, 0):
        to = on_chip(k, core)
        send(stage.at[rows_of(to), :], from_pair.at[k], a_send.at[k], a_recv.at[k], {"tensor": sib}).wait_recv()
        pair = stage[rows_of(to), :].astype(F32) + from_pair[k].astype(F32)
        if k:
            to_chip[k - 1] = pair.astype(BF16)
            copy = send(
                to_chip.at[k - 1], from_chip.at[k - 1], b_send.at[k - 1], b_recv.at[k - 1], {"tensor": to}
            )
            copy.start()
            pending.append(copy)

    dec_tail()

    y = pair + first[rows_of(t), :].astype(F32)
    for k in (1, 3, 2):
        send(
            to_chip.at[k - 1], from_chip.at[k - 1], b_send.at[k - 1], b_recv.at[k - 1], {"tensor": sib}
        ).wait_recv()
        y = y + from_chip[k - 1].astype(F32)
    result[...] = norm(y, gain2, shift2).astype(BF16)
    pre_out[rows_of(t), :] = result[:, pl.ds(pl.multiple_of(t * cols, cols), cols)]
    for d in range(1, n_tensor):
        to = lax.rem(t + d, n_tensor)
        copy = send(
            result.at[:, pl.ds(pl.multiple_of(to * cols, cols), cols)], pre_out.at[rows_of(t), :],
            o_send.at[d - 1], o_recv.at[d - 1], {"tensor": to},
        )
        copy.start()
        pending.append(copy)

    drain()

    for d in range(1, n_tensor):
        part = dec_term.at[lax.rem(t - d + n_tensor, n_tensor)]
        send(part, part, t_send.at[d - 1], t_recv.at[d - 1], {"tensor": sib}).wait_recv()
    dec_y = first[pl.ds(rows, TILE), :].astype(F32)[0:1, :] + jnp.sum(dec_term[:, 0, :], axis=0, keepdims=True)
    acc[pl.ds(rows, 8), :] = jnp.broadcast_to(norm(dec_y, gain2, shift2), (8, width))
    dec_out[...] = acc[pl.ds(rows, 8), pl.ds(pl.multiple_of(t * cols, cols), cols)][0:1, :].astype(BF16)

    for d in range(1, n_tensor):
        part = pre_out.at[rows_of(lax.rem(t - d + n_tensor, n_tensor)), :]
        send(part, part, o_send.at[d - 1], o_recv.at[d - 1], {"tensor": sib}).wait_recv()
    for copy in last:
        copy.wait_send()


def local(
    pre_tokens, dec_tokens, req_of, page_table, page_place, cache_lengths, cache_keys, cache_values,
    w_qkv, w_out, ln1_gain, ln1_bias, w_up, w_down, ln2_gain, ln2_bias,
    *, n_req, n_tensor,
):
    rows, cols = pre_tokens.shape
    width = w_qkv.shape[0]
    hidden = w_up.shape[1]
    n_keys = cache_keys.shape[0] * cache_keys.shape[1]
    share = rows // n_tensor
    n_chip = n_tensor // 2
    args = (
        pre_tokens, dec_tokens, req_of, page_table.T, page_place, cache_lengths,
        cache_keys.reshape(n_keys, cols), cache_values.reshape(n_keys, cols),
        jnp.transpose(w_qkv, (1, 0, 2)), w_out, ln1_gain, ln1_bias, w_up, w_down, ln2_gain, ln2_bias,
    )
    sem = pltpu.SemaphoreType.DMA
    vm = pltpu.VMEM
    scratch = [
        vm((rows + TILE, width), BF16),
        vm((rows + TILE, width), BF16),
        vm((rows + TILE, width), BF16),
        vm((3, width, cols), BF16),
        vm((width, width), BF16),
        vm((width, hidden), BF16),
        vm((hidden, width), BF16),
        vm((n_keys, cols), BF16),
        vm((n_keys, cols), BF16),
        vm((1, cols), BF16),
        vm(req_of.shape, jnp.int32),
        vm(page_table.shape[::-1], jnp.int32),
        vm(page_place.shape, jnp.int32),
        vm(cache_lengths.shape, jnp.int32),
        vm((width,), F32), vm((width,), F32), vm((width,), F32), vm((width,), F32),
        vm((n_req, 1, cols), F32),
        vm((n_req, 2, cols), F32),
        vm((n_req, 2, cols), F32),
        vm((rows + TILE, width), F32),
        vm((rows, width), BF16),
        vm((n_chip, share, width), BF16),
        vm((n_chip - 1, share, width), BF16),
        vm((n_chip - 1, share, width), BF16),
        vm((share, width), BF16),
        vm((n_tensor, 1, width), F32),
        sem((9,)), sem((9,)), pltpu.SemaphoreType.REGULAR,
        sem((9,)), sem((9,)), sem((7,)), sem((7,)), sem((9,)), sem((9,)), sem((7,)), sem((7,)),
        sem((10,)), sem((10,)),
        sem, sem, sem, sem,
        sem((4,)), sem((4,)), sem((3,)), sem((3,)), sem((7,)), sem((7,)), sem((7,)), sem((7,)),
    ]
    return pl.pallas_call(
        functools.partial(kernel, n_req=n_req, n_tensor=n_tensor),
        out_shape=(
            jax.ShapeDtypeStruct((rows, cols), BF16),
            jax.ShapeDtypeStruct((1, cols), BF16),
        ),
        in_specs=[pl.BlockSpec(memory_space=pltpu.HBM)] * len(args),
        out_specs=(
            pl.BlockSpec(memory_space=pltpu.VMEM),
            pl.BlockSpec(memory_space=pltpu.VMEM),
        ),
        scratch_shapes=scratch,
        compiler_params=pltpu.CompilerParams(
            collective_id=0, has_side_effects=True, vmem_limit_bytes=56 << 20
        ),
        name="layer",
    )(*args)


def solution(mesh):
    in_specs = (
        P("req", "tensor"),
        P("req", "tensor"),
        P(),
        P(),
        P(),
        P(),
        P("req", None, "tensor"),
        P("req", None, "tensor"),
        P(None, None, "tensor"),
        P("tensor", None),
        P(),
        P(),
        P(None, "tensor"),
        P("tensor", None),
        P(),
        P(),
    )
    out_specs = (P("req", "tensor"), P("req", "tensor"))
    body = functools.partial(local, n_req=mesh.shape["req"], n_tensor=mesh.shape["tensor"])
    return jax.shard_map(body, mesh=mesh, in_specs=in_specs, out_specs=out_specs, check_vma=False)
```

```python
import functools
import math

import jax
import jax.numpy as jnp
from jax import lax
from jax.experimental import pallas as pl
from jax.experimental.pallas import tpu as pltpu
from jax.sharding import PartitionSpec as P

MESH = pl.DeviceIdType.MESH
HD = 64
EPS = 1e-05
NEG = -1e30
F32 = jnp.float32
BF16 = jnp.bfloat16
TILE = 16


def dot(a, b, ca=1, cb=0):
    return lax.dot_general(a, b, (((ca,), (cb,)), ((), ())), preferred_element_type=F32)


def norm(total, gain, shift):
    mean = jnp.mean(total, axis=-1, keepdims=True)
    centered = total - mean
    var = jnp.mean(centered * centered, axis=-1, keepdims=True)
    return centered * lax.rsqrt(var + EPS) * gain + shift


def iota(shape, dim):
    return lax.broadcasted_iota(jnp.int32, shape, dim)


def kernel(
    pre_hbm, dec_hbm, req_hbm, table_hbm, place_hbm, len_hbm, keys_hbm, values_hbm,
    wqkv_hbm, wout_hbm, g1_hbm, b1_hbm, wup_hbm, wdown_hbm, g2_hbm, b2_hbm,
    pre_out, dec_out,
    x, ctx, first, wqkv, wout, wup, wdown, keys, values,
    dec_in, req, table, place, lens, g1, b1, g2, b2,
    q_all, partial, partial_all, acc, stage, from_pair, to_chip, from_chip, result, dec_term,
    local_sem, small_sem, near_in, ring_in,
    x_send, x_recv, d_send, d_recv, c_send, c_recv, e_send, e_recv, w_send, w_recv,
    q_send, q_recv, p_send, p_recv, a_send, a_recv, b_send, b_recv, t_send, t_recv, o_send, o_recv,
    *, n_req, n_tensor,
):
    rows = pre_hbm.shape[0]
    cols = pre_hbm.shape[1]
    width = cols * n_tensor
    pages = keys_hbm.shape[0] // 128
    n_chip = n_tensor // 2
    share = rows // n_tensor
    me = lax.axis_index("req")
    t = lax.axis_index("tensor")
    chip = t // 2
    core = lax.rem(t, 2)
    sib = t + 1 - 2 * core

    def on_chip(k, c):
        return lax.rem(chip + k, n_chip) * 2 + c

    def send(src, dst, ss, rs, dev):
        return pltpu.make_async_remote_copy(
            src_ref=src, dst_ref=dst, send_sem=ss, recv_sem=rs, device_id=dev, device_id_type=MESH
        )

    n_z = 16 if n_req % 16 == 0 else n_req
    n_y = n_req // n_z
    ys = sorted(range(n_y), key=lambda dy: -min(dy, n_y - dy))

    def each_peer(visit):
        my, mz = me // n_z, lax.rem(me, n_z)

        def visit_ring(dz, dys):
            for dy in dys:
                visit(lax.rem(my + dy, n_y) * n_z + lax.rem(mz + dz, n_z))

        def both_ways(i, carry):
            dz = n_z // 2 - 1 - i
            visit_ring(dz, ys)
            visit_ring(n_z - dz, ys)
            return carry

        visit_ring(n_z // 2, ys)
        lax.fori_loop(0, n_z // 2 - 1, both_ways, 0)
        visit_ring(0, [dy for dy in ys if dy])

    barrier = pltpu.get_barrier_semaphore()
    for d in range(1, n_tensor):
        pl.semaphore_signal(
            barrier, inc=1, device_id={"tensor": lax.rem(t + d, n_tensor)}, device_id_type=MESH
        )
    my, mz = me // n_z, lax.rem(me, n_z)
    columns = [lax.rem(my + dy, n_y) * n_z + mz for dy in ys if dy]
    reach = n_z // 4
    near = [
        my * n_z + lax.rem(mz + dz, n_z)
        for d in range(reach, 0, -1)
        for dz in (d, n_z - d)
    ]
    for to in near + columns:
        pl.semaphore_signal(barrier, inc=1, device_id={"req": to}, device_id_type=MESH)

    loads = [
        (dec_hbm, dec_in), (place_hbm, place), (table_hbm, table), (req_hbm, req), (len_hbm, lens),
        (g1_hbm, g1), (b1_hbm, b1), (g2_hbm, g2), (b2_hbm, b2),
    ]
    small = [pltpu.make_async_copy(a, b, small_sem.at[i]) for i, (a, b) in enumerate(loads)]
    small[0].start()

    def start_loads():
        for copy in big + small[1:]:
            copy.start()

    def own_cols(ref, lo, n):
        return ref.at[pl.ds(lo, n), pl.ds(pl.multiple_of(t * cols, cols), cols)]

    def cols_of(ref, lo, n, who):
        return ref.at[pl.ds(lo, n), pl.ds(pl.multiple_of(who * cols, cols), cols)]

    big = [
        pltpu.make_async_copy(wqkv_hbm, wqkv, local_sem.at[0]),
        pltpu.make_async_copy(pre_hbm, own_cols(x, 0, rows), local_sem.at[1]),
        pltpu.make_async_copy(keys_hbm, keys, local_sem.at[2]),
        pltpu.make_async_copy(values_hbm, values, local_sem.at[3]),
        pltpu.make_async_copy(
            wout_hbm, wout.at[pl.ds(pl.multiple_of(t * cols, cols), cols), :], local_sem.at[4]
        ),
        pltpu.make_async_copy(wup_hbm, wup, local_sem.at[5]),
        pltpu.make_async_copy(wdown_hbm, wdown, local_sem.at[6]),
    ]

    pending = []
    small[0].wait()
    tile = jnp.broadcast_to(dec_in[...].astype(F32), (TILE, cols)).astype(BF16)
    own_cols(x, rows, TILE)[...] = tile

    pl.semaphore_wait(barrier, n_tensor - 1 + len(near) + len(columns))
    for to in near[:2]:
        pl.semaphore_signal(near_in, inc=1, device_id={"req": to}, device_id_type=MESH)

    def tile_exchange(ref, ss, rs):
        out = []
        for d in sorted(range(1, n_tensor), key=lambda d: abs(d - n_tensor // 2)):
            copy = send(
                own_cols(ref, rows, TILE), own_cols(ref, rows, TILE), ss.at[d - 1], rs.at[d - 1],
                {"tensor": lax.rem(t + d, n_tensor)},
            )
            copy.start()
            out.append(copy)
        return out

    def tile_arrival(ref, ss, rs):
        for d in range(1, n_tensor):
            part = cols_of(ref, rows, TILE, lax.rem(t - d + n_tensor, n_tensor))
            send(part, part, ss.at[d - 1], rs.at[d - 1], {"tensor": sib}).wait_recv()

    def gather(own, region, ss, rs):
        def go(i, src, dst, dev):
            copy = send(src, dst, ss.at[i], rs.at[i], {"tensor": dev})
            copy.start()
            pending.append(copy)

        def arrived(i, ref):
            send(ref, ref, ss.at[i], rs.at[i], {"tensor": sib}).wait_recv()

        def begin():
            for k in (2, 1, 3):
                go(k, own, region(t), on_chip(k, core))
            go(0, own, region(t), sib)

        def forward(*ks):
            for k in ks:
                part = region(on_chip(n_chip - k, core))
                arrived(k, part)
                go(3 + k, part, part, sib)

        def end():
            arrived(0, region(sib))
            for k in (1, 3, 2):
                arrived(3 + k, region(on_chip(n_chip - k, 1 - core)))

        return begin, forward, end

    right, left, far = on_chip(1, core), on_chip(n_chip - 1, core), on_chip(2, core)

    def relay(own, region, ss, rs):
        def split(ref):
            n = ref.shape[0] // 2
            return ref.at[pl.ds(0, n), :], ref.at[pl.ds(n, n), :]

        def go(i, src, dst, dev):
            copy = send(src, dst, ss.at[i], rs.at[i], {"tensor": dev})
            copy.start()
            pending.append(copy)

        def arrived(i, ref):
            send(ref, ref, ss.at[i], rs.at[i], {"tensor": sib}).wait_recv()

        def begin():
            (own_top, own_bottom), (top, bottom) = split(own), split(region(t))
            go(1, own_top, top, right)
            go(2, own_bottom, bottom, left)
            go(3, own_bottom, bottom, right)
            go(4, own_top, top, left)
            go(0, own, region(t), sib)

        def onward():
            top, _ = split(region(left))
            arrived(1, top)
            go(5, top, top, right)
            _, bottom = split(region(right))
            arrived(2, bottom)
            go(6, bottom, bottom, left)

        def near():
            _, bottom = split(region(left))
            arrived(3, bottom)
            go(7, region(left), region(left), sib)
            top, _ = split(region(right))
            arrived(4, top)
            go(8, region(right), region(right), sib)

        def across():
            top, bottom = split(region(far))
            arrived(5, top)
            arrived(6, bottom)
            go(9, region(far), region(far), sib)

        def end():
            arrived(0, region(sib))
            arrived(7, region(on_chip(n_chip - 1, 1 - core)))
            arrived(8, region(on_chip(1, 1 - core)))
            arrived(9, region(on_chip(2, 1 - core)))

        return begin, onward, near, across, end

    def x_region(who):
        return cols_of(x, 0, rows, who)

    def c_region(who):
        return cols_of(ctx, 0, rows, who)

    def w_region(who):
        return wout.at[pl.ds(pl.multiple_of(who * cols, cols), cols), :]

    gather_x = gather(pre_hbm, x_region, x_send, x_recv)
    gather_w = relay(wout_hbm, w_region, w_send, w_recv)
    gather_c = gather(own_cols(ctx, 0, rows), c_region, c_send, c_recv)

    pending += tile_exchange(x, d_send, d_recv)
    gather_x[0]()
    gather_w[0]()
    start_loads()
    pl.semaphore_wait(near_in, 2)
    for to in columns:
        pl.semaphore_signal(ring_in, inc=1, device_id={"req": to}, device_id_type=MESH)

    for copy in small[1:]:
        copy.wait()
    n_page_ids = place.shape[0]
    n_r = req.shape[0]
    place_row = place[...].reshape(1, n_page_ids)
    held = place_row == (iota((TILE, n_page_ids), 0) + me * pages)
    page_id = jnp.sum(
        jnp.where(held, iota((TILE, n_page_ids), 1).astype(F32), 0.0), axis=1, keepdims=True
    )
    ids = table[...].astype(F32)
    in_page = jnp.clip(
        lens[...].reshape(1, n_r) - 128 * iota(table.shape, 0), 0, 128
    ).astype(F32)
    sub = iota((TILE, n_r), 0)
    tokens = jnp.zeros((TILE, n_r), F32)
    for s in range(pages):
        hit = jnp.sum(
            jnp.where(ids == page_id[s : s + 1, 0:1], in_page, 0.0), axis=0, keepdims=True
        )
        tokens = tokens + jnp.where(sub == s, hit, 0.0)
    req_row = jnp.broadcast_to(req[...].reshape(1, n_r).astype(F32), (8, n_r))
    lane_slot = lax.rem(iota((n_r, 2 * n_r), 1), n_r)
    twice = (iota((n_r, 2 * n_r), 0) == lane_slot).astype(F32).astype(BF16)
    req_twice = dot(req_row.astype(BF16), twice)[0:1, :]
    pick = (iota((n_r, 2 * n_r), 0).astype(F32) == req_twice).astype(F32).astype(BF16)
    in_slot = dot(tokens.astype(BF16), pick)

    lane = iota((1, cols), 1)
    low_head = lane < HD
    big[0].wait()
    tile_arrival(x, d_send, d_recv)
    x_dec = x[pl.ds(rows, TILE), :]
    q_dec = dot(x_dec, wqkv[0]).astype(BF16).astype(F32)[0:1, :]
    q_all[pl.ds(me, 1)] = q_dec.reshape(1, 1, cols)
    pl.semaphore_wait(ring_in, len(columns))
    each_peer(lambda to: send(q_all.at[me], q_all.at[me], q_send, q_recv, {"req": to}).start())
    k_dec = dot(x_dec, wqkv[1]).astype(BF16).astype(F32)[0:1, :]
    v_dec = dot(x_dec, wqkv[2]).astype(BF16).astype(F32)[0:1, :]

    gather_x[1](1, 3, 2)
    gather_w[1]()
    gather_x[2]()
    big[1].wait()
    x_pre = x[pl.ds(0, rows), :]
    q = dot(x_pre, wqkv[0])
    k = dot(x_pre, wqkv[1]).astype(BF16)
    v = dot(x_pre, wqkv[2]).astype(BF16)
    scale = 1.0 / math.sqrt(HD)
    causal = iota((rows, rows), 0) >= iota((rows, rows), 1)
    heads = []
    for h in range(2):
        qh = jnp.where(low_head if h == 0 else ~low_head, q, 0.0).astype(BF16)
        scores = jnp.where(causal, dot(qh, k, 1, 1) * scale, NEG)
        top = jnp.max(scores, axis=-1, keepdims=True)
        weights = jnp.where(causal, jnp.exp(scores - top), 0.0)
        total = jnp.sum(weights, axis=-1, keepdims=True)
        heads.append(dot(weights.astype(BF16), v) / total)
    own_cols(ctx, 0, rows)[...] = jnp.where(low_head, heads[0], heads[1]).astype(BF16)
    gather_c[0]()

    def q_wait(ref, sem):
        pltpu.make_async_copy(ref, ref, sem).wait()

    big[2].wait()
    big[3].wait()
    q_wait(q_all.at[pl.ds(0, n_req - 1)], q_recv)
    q_slots = q_all[:, 0, :]
    both = jnp.concatenate(
        [jnp.where(low_head, q_slots, 0.0), jnp.where(low_head, 0.0, q_slots)], axis=0
    ).astype(BF16)
    scores = dot(keys[...], both, 1, 1) * scale
    row_in_page = iota((128, 2 * n_req), 0).astype(F32)
    masks = [row_in_page < in_slot[s : s + 1, :] for s in range(pages)]
    parts = [
        jnp.where(masks[s], scores[s * 128 : (s + 1) * 128], NEG) for s in range(pages)
    ]
    top = functools.reduce(jnp.maximum, parts)
    top = jnp.max(top, axis=0, keepdims=True)
    parts = [jnp.where(m, jnp.exp(p - top), 0.0) for m, p in zip(masks, parts)]
    total = jnp.sum(functools.reduce(jnp.add, parts), axis=0, keepdims=True)
    weights = jnp.concatenate(parts, axis=0).astype(BF16)
    summed = dot(weights, values[...], 0, 0)
    diag = iota((2 * n_req, 2 * n_req), 0) == iota((2 * n_req, 2 * n_req), 1)

    def per_slot(row):
        column = jnp.sum(jnp.where(diag, row, 0.0), axis=1, keepdims=True)
        return jnp.where(low_head, column[:n_req], column[n_req:])

    first_half = lax.rem(lane, HD) < HD // 2
    partial[:, 0, :] = jnp.where(low_head, summed[:n_req], summed[n_req:])
    partial[:, 1, :] = jnp.where(first_half, per_slot(top), per_slot(total))
    partial_all[pl.ds(me, 1)] = partial[pl.ds(me, 1)]
    each_peer(lambda to: send(partial.at[to], partial_all.at[me], p_send, p_recv, {"req": to}).start())

    gather_w[2]()
    gather_c[1](1, 3, 2)
    gather_w[3]()
    gain1 = g1[...].reshape(1, width)
    shift1 = b1[...].reshape(1, width)
    gain2 = g2[...].reshape(1, width)
    shift2 = b2[...].reshape(1, width)

    def feed_forward(lo, n, chunk):
        acc[pl.ds(lo, n), :] = dot(ctx[pl.ds(lo, n), :], wout[...])
        for at in range(lo, lo + n, chunk):
            total = x[pl.ds(at, chunk), :].astype(F32) + acc[pl.ds(at, chunk), :]
            first[pl.ds(at, chunk), :] = norm(total, gain1, shift1).astype(BF16)
        up = dot(first[pl.ds(lo, n), :], wup[...])
        hidden = (0.5 * up * (1.0 + lax.erf(up * (1.0 / math.sqrt(2.0))))).astype(BF16)
        return dot(hidden, wdown[...])

    def dec_merge():
        q_wait(partial_all.at[pl.ds(0, n_req - 1)], p_recv)
        sums = partial_all[:, 0, :]
        stats = partial_all[:, 1, :]
        tops = jnp.where(first_half, stats, pltpu.roll(stats, HD // 2, 1))
        totals = jnp.where(first_half, pltpu.roll(stats, cols - HD // 2, 1), stats)
        qk = q_dec * k_dec
        own_score = scale * jnp.where(
            low_head,
            jnp.sum(jnp.where(low_head, qk, 0.0), axis=1, keepdims=True),
            jnp.sum(jnp.where(low_head, 0.0, qk), axis=1, keepdims=True),
        )
        best = jnp.maximum(jnp.max(tops, axis=0, keepdims=True), own_score)
        factor = jnp.exp(tops - best)
        own_weight = jnp.exp(own_score - best)
        dec_total = jnp.sum(totals * factor, axis=0, keepdims=True) + own_weight
        dec_sum = jnp.sum(sums * factor, axis=0, keepdims=True) + own_weight * v_dec
        own_cols(ctx, rows, TILE)[...] = jnp.broadcast_to(dec_sum / dec_total, (TILE, cols)).astype(BF16)
        pending.extend(tile_exchange(ctx, e_send, e_recv))

    last = []

    def dec_tail():
        tile_arrival(ctx, e_send, e_recv)
        term = feed_forward(rows, TILE, TILE)[0:1, :].astype(BF16).astype(F32)
        dec_term[pl.ds(t, 1)] = term.reshape(1, 1, width)
        for d in range(1, n_tensor):
            copy = send(
                dec_term.at[t], dec_term.at[t], t_send.at[d - 1], t_recv.at[d - 1],
                {"tensor": lax.rem(t + d, n_tensor)},
            )
            copy.start()
            last.append(copy)

    def drain():
        q_wait(q_all.at[pl.ds(0, n_req - 1)], q_send)
        q_wait(partial.at[pl.ds(0, n_req - 1)], p_send)
        for copy in pending:
            copy.wait_send()

    big[4].wait()
    big[5].wait()
    big[6].wait()
    gather_c[2]()
    gather_w[4]()
    stage[...] = feed_forward(0, rows, 64).astype(BF16)

    def rows_of(who):
        return pl.ds(pl.multiple_of(who * share, share), share)

    for k in range(n_chip):
        to = on_chip(k, 1 - core)
        copy = send(stage.at[rows_of(to), :], from_pair.at[k], a_send.at[k], a_recv.at[k], {"tensor": sib})
        copy.start()
        pending.append(copy)
    dec_merge()
    for k in (2, 1, 3, 0):
        to = on_chip(k, core)
        send(stage.at[rows_of(to), :], from_pair.at[k], a_send.at[k], a_recv.at[k], {"tensor": sib}).wait_recv()
        pair = stage[rows_of(to), :].astype(F32) + from_pair[k].astype(F32)
        if k:
            to_chip[k - 1] = pair.astype(BF16)
            copy = send(
                to_chip.at[k - 1], from_chip.at[k - 1], b_send.at[k - 1], b_recv.at[k - 1], {"tensor": to}
            )
            copy.start()
            pending.append(copy)

    dec_tail()

    y = pair + first[rows_of(t), :].astype(F32)
    for k in (1, 3, 2):
        send(
            to_chip.at[k - 1], from_chip.at[k - 1], b_send.at[k - 1], b_recv.at[k - 1], {"tensor": sib}
        ).wait_recv()
        y = y + from_chip[k - 1].astype(F32)
    result[...] = norm(y, gain2, shift2).astype(BF16)
    pre_out[rows_of(t), :] = result[:, pl.ds(pl.multiple_of(t * cols, cols), cols)]
    for d in range(1, n_tensor):
        to = lax.rem(t + d, n_tensor)
        copy = send(
            result.at[:, pl.ds(pl.multiple_of(to * cols, cols), cols)], pre_out.at[rows_of(t), :],
            o_send.at[d - 1], o_recv.at[d - 1], {"tensor": to},
        )
        copy.start()
        pending.append(copy)

    drain()

    for d in range(1, n_tensor):
        part = dec_term.at[lax.rem(t - d + n_tensor, n_tensor)]
        send(part, part, t_send.at[d - 1], t_recv.at[d - 1], {"tensor": sib}).wait_recv()
    dec_y = first[pl.ds(rows, TILE), :].astype(F32)[0:1, :] + jnp.sum(dec_term[:, 0, :], axis=0, keepdims=True)
    acc[pl.ds(rows, 8), :] = jnp.broadcast_to(norm(dec_y, gain2, shift2), (8, width))
    dec_out[...] = acc[pl.ds(rows, 8), pl.ds(pl.multiple_of(t * cols, cols), cols)][0:1, :].astype(BF16)

    for d in range(1, n_tensor):
        part = pre_out.at[rows_of(lax.rem(t - d + n_tensor, n_tensor)), :]
        send(part, part, o_send.at[d - 1], o_recv.at[d - 1], {"tensor": sib}).wait_recv()
    for copy in last:
        copy.wait_send()


def local(
    pre_tokens, dec_tokens, req_of, page_table, page_place, cache_lengths, cache_keys, cache_values,
    w_qkv, w_out, ln1_gain, ln1_bias, w_up, w_down, ln2_gain, ln2_bias,
    *, n_req, n_tensor,
):
    rows, cols = pre_tokens.shape
    width = w_qkv.shape[0]
    hidden = w_up.shape[1]
    n_keys = cache_keys.shape[0] * cache_keys.shape[1]
    share = rows // n_tensor
    n_chip = n_tensor // 2
    args = (
        pre_tokens, dec_tokens, req_of, page_table.T, page_place, cache_lengths,
        cache_keys.reshape(n_keys, cols), cache_values.reshape(n_keys, cols),
        jnp.transpose(w_qkv, (1, 0, 2)), w_out, ln1_gain, ln1_bias, w_up, w_down, ln2_gain, ln2_bias,
    )
    sem = pltpu.SemaphoreType.DMA
    vm = pltpu.VMEM
    scratch = [
        vm((rows + TILE, width), BF16),
        vm((rows + TILE, width), BF16),
        vm((rows + TILE, width), BF16),
        vm((3, width, cols), BF16),
        vm((width, width), BF16),
        vm((width, hidden), BF16),
        vm((hidden, width), BF16),
        vm((n_keys, cols), BF16),
        vm((n_keys, cols), BF16),
        vm((1, cols), BF16),
        vm(req_of.shape, jnp.int32),
        vm(page_table.shape[::-1], jnp.int32),
        vm(page_place.shape, jnp.int32),
        vm(cache_lengths.shape, jnp.int32),
        vm((width,), F32), vm((width,), F32), vm((width,), F32), vm((width,), F32),
        vm((n_req, 1, cols), F32),
        vm((n_req, 2, cols), F32),
        vm((n_req, 2, cols), F32),
        vm((rows + TILE, width), F32),
        vm((rows, width), BF16),
        vm((n_chip, share, width), BF16),
        vm((n_chip - 1, share, width), BF16),
        vm((n_chip - 1, share, width), BF16),
        vm((share, width), BF16),
        vm((n_tensor, 1, width), F32),
        sem((9,)), sem((9,)), pltpu.SemaphoreType.REGULAR, pltpu.SemaphoreType.REGULAR,
        sem((9,)), sem((9,)), sem((7,)), sem((7,)), sem((9,)), sem((9,)), sem((7,)), sem((7,)),
        sem((10,)), sem((10,)),
        sem, sem, sem, sem,
        sem((4,)), sem((4,)), sem((3,)), sem((3,)), sem((7,)), sem((7,)), sem((7,)), sem((7,)),
    ]
    return pl.pallas_call(
        functools.partial(kernel, n_req=n_req, n_tensor=n_tensor),
        out_shape=(
            jax.ShapeDtypeStruct((rows, cols), BF16),
            jax.ShapeDtypeStruct((1, cols), BF16),
        ),
        in_specs=[pl.BlockSpec(memory_space=pltpu.HBM)] * len(args),
        out_specs=(
            pl.BlockSpec(memory_space=pltpu.VMEM),
            pl.BlockSpec(memory_space=pltpu.VMEM),
        ),
        scratch_shapes=scratch,
        compiler_params=pltpu.CompilerParams(
            collective_id=0, has_side_effects=True, vmem_limit_bytes=56 << 20
        ),
        name="layer",
    )(*args)


def solution(mesh):
    in_specs = (
        P("req", "tensor"),
        P("req", "tensor"),
        P(),
        P(),
        P(),
        P(),
        P("req", None, "tensor"),
        P("req", None, "tensor"),
        P(None, None, "tensor"),
        P("tensor", None),
        P(),
        P(),
        P(None, "tensor"),
        P("tensor", None),
        P(),
        P(),
    )
    out_specs = (P("req", "tensor"), P("req", "tensor"))
    body = functools.partial(local, n_req=mesh.shape["req"], n_tensor=mesh.shape["tensor"])
    return jax.shard_map(body, mesh=mesh, in_specs=in_specs, out_specs=out_specs, check_vma=False)
```

```python
import functools
import math

import jax
import jax.numpy as jnp
from jax import lax
from jax.experimental import pallas as pl
from jax.experimental.pallas import tpu as pltpu
from jax.sharding import PartitionSpec as P

MESH = pl.DeviceIdType.MESH
HD = 64
EPS = 1e-05
NEG = -1e30
F32 = jnp.float32
BF16 = jnp.bfloat16
TILE = 16


def dot(a, b, ca=1, cb=0):
    return lax.dot_general(a, b, (((ca,), (cb,)), ((), ())), preferred_element_type=F32)


def norm(total, gain, shift):
    mean = jnp.mean(total, axis=-1, keepdims=True)
    centered = total - mean
    var = jnp.mean(centered * centered, axis=-1, keepdims=True)
    return centered * lax.rsqrt(var + EPS) * gain + shift


def iota(shape, dim):
    return lax.broadcasted_iota(jnp.int32, shape, dim)


def kernel(
    pre_hbm, dec_hbm, req_hbm, table_hbm, place_hbm, len_hbm, keys_hbm, values_hbm,
    wqkv_hbm, wout_hbm, g1_hbm, b1_hbm, wup_hbm, wdown_hbm, g2_hbm, b2_hbm,
    pre_out, dec_out,
    x, ctx, first, wqkv, wout, wup, wdown, keys, values,
    dec_in, req, table, place, lens, g1, b1, g2, b2,
    q_all, partial, partial_all, acc, stage, from_pair, to_chip, from_chip, result, dec_term,
    local_sem, small_sem, near_in, ring_in,
    x_send, x_recv, d_send, d_recv, c_send, c_recv, e_send, e_recv, w_send, w_recv,
    q_send, q_recv, p_send, p_recv, a_send, a_recv, b_send, b_recv, t_send, t_recv, o_send, o_recv,
    *, n_req, n_tensor,
):
    rows = pre_hbm.shape[0]
    cols = pre_hbm.shape[1]
    width = cols * n_tensor
    pages = keys_hbm.shape[0] // 128
    n_chip = n_tensor // 2
    share = rows // n_tensor
    me = lax.axis_index("req")
    t = lax.axis_index("tensor")
    chip = t // 2
    core = lax.rem(t, 2)
    sib = t + 1 - 2 * core

    def on_chip(k, c):
        return lax.rem(chip + k, n_chip) * 2 + c

    def send(src, dst, ss, rs, dev):
        return pltpu.make_async_remote_copy(
            src_ref=src, dst_ref=dst, send_sem=ss, recv_sem=rs, device_id=dev, device_id_type=MESH
        )

    n_z = 16 if n_req % 16 == 0 else n_req
    n_y = n_req // n_z
    ys = sorted(range(n_y), key=lambda dy: -min(dy, n_y - dy))

    def each_peer(visit):
        my, mz = me // n_z, lax.rem(me, n_z)

        def visit_ring(dz, dys):
            for dy in dys:
                visit(lax.rem(my + dy, n_y) * n_z + lax.rem(mz + dz, n_z))

        def both_ways(i, carry):
            dz = n_z // 2 - 1 - i
            visit_ring(dz, ys)
            visit_ring(n_z - dz, ys)
            return carry

        visit_ring(n_z // 2, ys)
        lax.fori_loop(0, n_z // 2 - 1, both_ways, 0)
        visit_ring(0, [dy for dy in ys if dy])

    barrier = pltpu.get_barrier_semaphore()
    for d in range(1, n_tensor):
        pl.semaphore_signal(
            barrier, inc=1, device_id={"tensor": lax.rem(t + d, n_tensor)}, device_id_type=MESH
        )
    my, mz = me // n_z, lax.rem(me, n_z)
    columns = [lax.rem(my + dy, n_y) * n_z + mz for dy in ys if dy]
    reach = n_z // 4
    near = [
        my * n_z + lax.rem(mz + dz, n_z)
        for d in range(reach, 0, -1)
        for dz in (d, n_z - d)
    ]
    for to in near + columns:
        pl.semaphore_signal(barrier, inc=1, device_id={"req": to}, device_id_type=MESH)

    loads = [
        (dec_hbm, dec_in), (place_hbm, place), (table_hbm, table), (req_hbm, req), (len_hbm, lens),
        (g1_hbm, g1), (b1_hbm, b1), (g2_hbm, g2), (b2_hbm, b2),
    ]
    small = [pltpu.make_async_copy(a, b, small_sem.at[i]) for i, (a, b) in enumerate(loads)]
    small[0].start()

    def start_loads():
        for copy in big + small[1:]:
            copy.start()

    def own_cols(ref, lo, n):
        return ref.at[pl.ds(lo, n), pl.ds(pl.multiple_of(t * cols, cols), cols)]

    def cols_of(ref, lo, n, who):
        return ref.at[pl.ds(lo, n), pl.ds(pl.multiple_of(who * cols, cols), cols)]

    big = [
        pltpu.make_async_copy(wqkv_hbm, wqkv, local_sem.at[0]),
        pltpu.make_async_copy(pre_hbm, own_cols(x, 0, rows), local_sem.at[1]),
        pltpu.make_async_copy(keys_hbm, keys, local_sem.at[2]),
        pltpu.make_async_copy(values_hbm, values, local_sem.at[3]),
        pltpu.make_async_copy(
            wout_hbm, wout.at[pl.ds(pl.multiple_of(t * cols, cols), cols), :], local_sem.at[4]
        ),
        pltpu.make_async_copy(wup_hbm, wup, local_sem.at[5]),
        pltpu.make_async_copy(wdown_hbm, wdown, local_sem.at[6]),
    ]

    pending = []
    small[0].wait()
    tile = jnp.broadcast_to(dec_in[...].astype(F32), (TILE, cols)).astype(BF16)
    own_cols(x, rows, TILE)[...] = tile

    pl.semaphore_wait(barrier, n_tensor - 1 + len(near) + len(columns))
    for to in near[:2]:
        pl.semaphore_signal(near_in, inc=1, device_id={"req": to}, device_id_type=MESH)

    def tile_exchange(ref, ss, rs):
        out = []
        for d in sorted(range(1, n_tensor), key=lambda d: abs(d - n_tensor // 2)):
            copy = send(
                own_cols(ref, rows, TILE), own_cols(ref, rows, TILE), ss.at[d - 1], rs.at[d - 1],
                {"tensor": lax.rem(t + d, n_tensor)},
            )
            copy.start()
            out.append(copy)
        return out

    def tile_arrival(ref, ss, rs):
        for d in range(1, n_tensor):
            part = cols_of(ref, rows, TILE, lax.rem(t - d + n_tensor, n_tensor))
            send(part, part, ss.at[d - 1], rs.at[d - 1], {"tensor": sib}).wait_recv()

    def gather(own, region, ss, rs):
        def go(i, src, dst, dev):
            copy = send(src, dst, ss.at[i], rs.at[i], {"tensor": dev})
            copy.start()
            pending.append(copy)

        def arrived(i, ref):
            send(ref, ref, ss.at[i], rs.at[i], {"tensor": sib}).wait_recv()

        def begin():
            for k in (2, 1, 3):
                go(k, own, region(t), on_chip(k, core))
            go(0, own, region(t), sib)

        def forward(*ks):
            for k in ks:
                part = region(on_chip(n_chip - k, core))
                arrived(k, part)
                go(3 + k, part, part, sib)

        def end():
            arrived(0, region(sib))
            for k in (1, 3, 2):
                arrived(3 + k, region(on_chip(n_chip - k, 1 - core)))

        return begin, forward, end

    right, left, far = on_chip(1, core), on_chip(n_chip - 1, core), on_chip(2, core)

    def relay(own, region, ss, rs):
        def split(ref):
            n = ref.shape[0] // 2
            return ref.at[pl.ds(0, n), :], ref.at[pl.ds(n, n), :]

        def go(i, src, dst, dev):
            copy = send(src, dst, ss.at[i], rs.at[i], {"tensor": dev})
            copy.start()
            pending.append(copy)

        def arrived(i, ref):
            send(ref, ref, ss.at[i], rs.at[i], {"tensor": sib}).wait_recv()

        def begin():
            (own_top, own_bottom), (top, bottom) = split(own), split(region(t))
            go(1, own_top, top, right)
            go(2, own_bottom, bottom, left)
            go(3, own_bottom, bottom, right)
            go(4, own_top, top, left)
            go(0, own, region(t), sib)

        def onward():
            top, _ = split(region(left))
            arrived(1, top)
            go(5, top, top, right)
            _, bottom = split(region(right))
            arrived(2, bottom)
            go(6, bottom, bottom, left)

        def near():
            _, bottom = split(region(left))
            arrived(3, bottom)
            go(7, region(left), region(left), sib)
            top, _ = split(region(right))
            arrived(4, top)
            go(8, region(right), region(right), sib)

        def across():
            top, bottom = split(region(far))
            arrived(5, top)
            arrived(6, bottom)
            go(9, region(far), region(far), sib)

        def end():
            arrived(0, region(sib))
            arrived(7, region(on_chip(n_chip - 1, 1 - core)))
            arrived(8, region(on_chip(1, 1 - core)))
            arrived(9, region(on_chip(2, 1 - core)))

        return begin, onward, near, across, end

    def x_region(who):
        return cols_of(x, 0, rows, who)

    def c_region(who):
        return cols_of(ctx, 0, rows, who)

    def w_region(who):
        return wout.at[pl.ds(pl.multiple_of(who * cols, cols), cols), :]

    gather_x = gather(pre_hbm, x_region, x_send, x_recv)
    gather_w = relay(wout_hbm, w_region, w_send, w_recv)
    gather_c = gather(own_cols(ctx, 0, rows), c_region, c_send, c_recv)

    pending += tile_exchange(x, d_send, d_recv)
    gather_x[0]()
    gather_w[0]()
    start_loads()
    pl.semaphore_wait(near_in, 2)
    for to in columns:
        pl.semaphore_signal(ring_in, inc=1, device_id={"req": to}, device_id_type=MESH)

    for copy in small[1:]:
        copy.wait()
    n_page_ids = place.shape[0]
    n_r = req.shape[0]
    place_row = place[...].reshape(1, n_page_ids)
    held = place_row == (iota((TILE, n_page_ids), 0) + me * pages)
    page_id = jnp.sum(
        jnp.where(held, iota((TILE, n_page_ids), 1).astype(F32), 0.0), axis=1, keepdims=True
    )
    ids = table[...].astype(F32)
    in_page = jnp.clip(
        lens[...].reshape(1, n_r) - 128 * iota(table.shape, 0), 0, 128
    ).astype(F32)
    sub = iota((TILE, n_r), 0)
    tokens = jnp.zeros((TILE, n_r), F32)
    for s in range(pages):
        hit = jnp.sum(
            jnp.where(ids == page_id[s : s + 1, 0:1], in_page, 0.0), axis=0, keepdims=True
        )
        tokens = tokens + jnp.where(sub == s, hit, 0.0)
    req_row = jnp.broadcast_to(req[...].reshape(1, n_r).astype(F32), (8, n_r))
    lane_slot = lax.rem(iota((n_r, 2 * n_r), 1), n_r)
    twice = (iota((n_r, 2 * n_r), 0) == lane_slot).astype(F32).astype(BF16)
    req_twice = dot(req_row.astype(BF16), twice)[0:1, :]
    pick = (iota((n_r, 2 * n_r), 0).astype(F32) == req_twice).astype(F32).astype(BF16)
    in_slot = dot(tokens.astype(BF16), pick)

    lane = iota((1, cols), 1)
    low_head = lane < HD
    big[0].wait()
    tile_arrival(x, d_send, d_recv)
    x_dec = x[pl.ds(rows, TILE), :]
    q_dec = dot(x_dec, wqkv[0]).astype(BF16).astype(F32)[0:1, :]
    q_all[pl.ds(me, 1)] = q_dec.reshape(1, 1, cols)
    pl.semaphore_wait(ring_in, len(columns))
    each_peer(lambda to: send(q_all.at[me], q_all.at[me], q_send, q_recv, {"req": to}).start())
    k_dec = dot(x_dec, wqkv[1]).astype(BF16).astype(F32)[0:1, :]
    v_dec = dot(x_dec, wqkv[2]).astype(BF16).astype(F32)[0:1, :]

    gather_x[1](1, 3, 2)
    gather_w[1]()
    gather_x[2]()
    big[1].wait()
    x_pre = x[pl.ds(0, rows), :]
    q = dot(x_pre, wqkv[0])
    k = dot(x_pre, wqkv[1]).astype(BF16)
    v = dot(x_pre, wqkv[2]).astype(BF16)
    scale = 1.0 / math.sqrt(HD)
    causal = iota((rows, rows), 0) >= iota((rows, rows), 1)
    heads = []
    for h in range(2):
        qh = jnp.where(low_head if h == 0 else ~low_head, q, 0.0).astype(BF16)
        scores = jnp.where(causal, dot(qh, k, 1, 1) * scale, NEG)
        top = jnp.max(scores, axis=-1, keepdims=True)
        weights = jnp.where(causal, jnp.exp(scores - top), 0.0)
        total = jnp.sum(weights, axis=-1, keepdims=True)
        heads.append(dot(weights.astype(BF16), v) / total)
    own_cols(ctx, 0, rows)[...] = jnp.where(low_head, heads[0], heads[1]).astype(BF16)
    gather_c[0]()

    def q_wait(ref, sem):
        pltpu.make_async_copy(ref, ref, sem).wait()

    big[2].wait()
    big[3].wait()
    q_wait(q_all.at[pl.ds(0, n_req - 1)], q_recv)
    q_slots = q_all[:, 0, :]
    both = jnp.concatenate(
        [jnp.where(low_head, q_slots, 0.0), jnp.where(low_head, 0.0, q_slots)], axis=0
    ).astype(BF16)
    scores = dot(keys[...], both, 1, 1) * scale
    row_in_page = iota((128, 2 * n_req), 0).astype(F32)
    masks = [row_in_page < in_slot[s : s + 1, :] for s in range(pages)]
    parts = [
        jnp.where(masks[s], scores[s * 128 : (s + 1) * 128], NEG) for s in range(pages)
    ]
    top = functools.reduce(jnp.maximum, parts)
    top = jnp.max(top, axis=0, keepdims=True)
    parts = [jnp.where(m, jnp.exp(p - top), 0.0) for m, p in zip(masks, parts)]
    total = jnp.sum(functools.reduce(jnp.add, parts), axis=0, keepdims=True)
    weights = jnp.concatenate(parts, axis=0).astype(BF16)
    summed = dot(weights, values[...], 0, 0)
    diag = iota((2 * n_req, 2 * n_req), 0) == iota((2 * n_req, 2 * n_req), 1)

    def per_slot(row):
        column = jnp.sum(jnp.where(diag, row, 0.0), axis=1, keepdims=True)
        return jnp.where(low_head, column[:n_req], column[n_req:])

    first_half = lax.rem(lane, HD) < HD // 2
    partial[:, 0, :] = jnp.where(low_head, summed[:n_req], summed[n_req:])
    partial[:, 1, :] = jnp.where(first_half, per_slot(top), per_slot(total))
    partial_all[pl.ds(me, 1)] = partial[pl.ds(me, 1)]
    each_peer(lambda to: send(partial.at[to], partial_all.at[me], p_send, p_recv, {"req": to}).start())

    gather_w[2]()
    gather_c[1](1, 3, 2)
    gather_w[3]()
    gain1 = g1[...].reshape(1, width)
    shift1 = b1[...].reshape(1, width)
    gain2 = g2[...].reshape(1, width)
    shift2 = b2[...].reshape(1, width)

    def feed_forward(lo, n, chunk):
        acc[pl.ds(lo, n), :] = dot(ctx[pl.ds(lo, n), :], wout[...])
        for at in range(lo, lo + n, chunk):
            total = x[pl.ds(at, chunk), :].astype(F32) + acc[pl.ds(at, chunk), :]
            first[pl.ds(at, chunk), :] = norm(total, gain1, shift1).astype(BF16)
        up = dot(first[pl.ds(lo, n), :], wup[...])
        hidden = (0.5 * up * (1.0 + lax.erf(up * (1.0 / math.sqrt(2.0))))).astype(BF16)
        return dot(hidden, wdown[...])

    def dec_merge():
        q_wait(partial_all.at[pl.ds(0, n_req - 1)], p_recv)
        sums = partial_all[:, 0, :]
        stats = partial_all[:, 1, :]
        tops = jnp.where(first_half, stats, pltpu.roll(stats, HD // 2, 1))
        totals = jnp.where(first_half, pltpu.roll(stats, cols - HD // 2, 1), stats)
        qk = q_dec * k_dec
        own_score = scale * jnp.where(
            low_head,
            jnp.sum(jnp.where(low_head, qk, 0.0), axis=1, keepdims=True),
            jnp.sum(jnp.where(low_head, 0.0, qk), axis=1, keepdims=True),
        )
        best = jnp.maximum(jnp.max(tops, axis=0, keepdims=True), own_score)
        factor = jnp.exp(tops - best)
        own_weight = jnp.exp(own_score - best)
        dec_total = jnp.sum(totals * factor, axis=0, keepdims=True) + own_weight
        dec_sum = jnp.sum(sums * factor, axis=0, keepdims=True) + own_weight * v_dec
        own_cols(ctx, rows, TILE)[...] = jnp.broadcast_to(dec_sum / dec_total, (TILE, cols)).astype(BF16)
        pending.extend(tile_exchange(ctx, e_send, e_recv))

    last = []

    def dec_tail():
        tile_arrival(ctx, e_send, e_recv)
        term = feed_forward(rows, TILE, TILE)[0:1, :].astype(BF16).astype(F32)
        dec_term[pl.ds(t, 1)] = term.reshape(1, 1, width)
        for d in range(1, n_tensor):
            copy = send(
                dec_term.at[t], dec_term.at[t], t_send.at[d - 1], t_recv.at[d - 1],
                {"tensor": lax.rem(t + d, n_tensor)},
            )
            copy.start()
            last.append(copy)

    def drain():
        q_wait(q_all.at[pl.ds(0, n_req - 1)], q_send)
        q_wait(partial.at[pl.ds(0, n_req - 1)], p_send)
        for copy in pending:
            copy.wait_send()

    big[4].wait()
    big[5].wait()
    big[6].wait()
    gather_c[2]()
    gather_w[4]()
    stage[...] = feed_forward(0, rows, 64).astype(BF16)

    def rows_of(who):
        return pl.ds(pl.multiple_of(who * share, share), share)

    for k in range(n_chip):
        to = on_chip(k, 1 - core)
        copy = send(stage.at[rows_of(to), :], from_pair.at[k], a_send.at[k], a_recv.at[k], {"tensor": sib})
        copy.start()
        pending.append(copy)
    for k in (2, 1, 3, 0):
        to = on_chip(k, core)
        send(stage.at[rows_of(to), :], from_pair.at[k], a_send.at[k], a_recv.at[k], {"tensor": sib}).wait_recv()
        pair = stage[rows_of(to), :].astype(F32) + from_pair[k].astype(F32)
        if k:
            to_chip[k - 1] = pair.astype(BF16)
            copy = send(
                to_chip.at[k - 1], from_chip.at[k - 1], b_send.at[k - 1], b_recv.at[k - 1], {"tensor": to}
            )
            copy.start()
            pending.append(copy)

    dec_merge()
    dec_tail()

    y = pair + first[rows_of(t), :].astype(F32)
    for k in (1, 3, 2):
        send(
            to_chip.at[k - 1], from_chip.at[k - 1], b_send.at[k - 1], b_recv.at[k - 1], {"tensor": sib}
        ).wait_recv()
        y = y + from_chip[k - 1].astype(F32)
    result[...] = norm(y, gain2, shift2).astype(BF16)
    pre_out[rows_of(t), :] = result[:, pl.ds(pl.multiple_of(t * cols, cols), cols)]
    for d in range(1, n_tensor):
        to = lax.rem(t + d, n_tensor)
        copy = send(
            result.at[:, pl.ds(pl.multiple_of(to * cols, cols), cols)], pre_out.at[rows_of(t), :],
            o_send.at[d - 1], o_recv.at[d - 1], {"tensor": to},
        )
        copy.start()
        pending.append(copy)

    drain()

    for d in range(1, n_tensor):
        part = dec_term.at[lax.rem(t - d + n_tensor, n_tensor)]
        send(part, part, t_send.at[d - 1], t_recv.at[d - 1], {"tensor": sib}).wait_recv()
    dec_y = first[pl.ds(rows, TILE), :].astype(F32)[0:1, :] + jnp.sum(dec_term[:, 0, :], axis=0, keepdims=True)
    acc[pl.ds(rows, 8), :] = jnp.broadcast_to(norm(dec_y, gain2, shift2), (8, width))
    dec_out[...] = acc[pl.ds(rows, 8), pl.ds(pl.multiple_of(t * cols, cols), cols)][0:1, :].astype(BF16)

    for d in range(1, n_tensor):
        part = pre_out.at[rows_of(lax.rem(t - d + n_tensor, n_tensor)), :]
        send(part, part, o_send.at[d - 1], o_recv.at[d - 1], {"tensor": sib}).wait_recv()
    for copy in last:
        copy.wait_send()


def local(
    pre_tokens, dec_tokens, req_of, page_table, page_place, cache_lengths, cache_keys, cache_values,
    w_qkv, w_out, ln1_gain, ln1_bias, w_up, w_down, ln2_gain, ln2_bias,
    *, n_req, n_tensor,
):
    rows, cols = pre_tokens.shape
    width = w_qkv.shape[0]
    hidden = w_up.shape[1]
    n_keys = cache_keys.shape[0] * cache_keys.shape[1]
    share = rows // n_tensor
    n_chip = n_tensor // 2
    args = (
        pre_tokens, dec_tokens, req_of, page_table.T, page_place, cache_lengths,
        cache_keys.reshape(n_keys, cols), cache_values.reshape(n_keys, cols),
        jnp.transpose(w_qkv, (1, 0, 2)), w_out, ln1_gain, ln1_bias, w_up, w_down, ln2_gain, ln2_bias,
    )
    sem = pltpu.SemaphoreType.DMA
    vm = pltpu.VMEM
    scratch = [
        vm((rows + TILE, width), BF16),
        vm((rows + TILE, width), BF16),
        vm((rows + TILE, width), BF16),
        vm((3, width, cols), BF16),
        vm((width, width), BF16),
        vm((width, hidden), BF16),
        vm((hidden, width), BF16),
        vm((n_keys, cols), BF16),
        vm((n_keys, cols), BF16),
        vm((1, cols), BF16),
        vm(req_of.shape, jnp.int32),
        vm(page_table.shape[::-1], jnp.int32),
        vm(page_place.shape, jnp.int32),
        vm(cache_lengths.shape, jnp.int32),
        vm((width,), F32), vm((width,), F32), vm((width,), F32), vm((width,), F32),
        vm((n_req, 1, cols), F32),
        vm((n_req, 2, cols), F32),
        vm((n_req, 2, cols), F32),
        vm((rows + TILE, width), F32),
        vm((rows, width), BF16),
        vm((n_chip, share, width), BF16),
        vm((n_chip - 1, share, width), BF16),
        vm((n_chip - 1, share, width), BF16),
        vm((share, width), BF16),
        vm((n_tensor, 1, width), F32),
        sem((9,)), sem((9,)), pltpu.SemaphoreType.REGULAR, pltpu.SemaphoreType.REGULAR,
        sem((9,)), sem((9,)), sem((7,)), sem((7,)), sem((9,)), sem((9,)), sem((7,)), sem((7,)),
        sem((10,)), sem((10,)),
        sem, sem, sem, sem,
        sem((4,)), sem((4,)), sem((3,)), sem((3,)), sem((7,)), sem((7,)), sem((7,)), sem((7,)),
    ]
    return pl.pallas_call(
        functools.partial(kernel, n_req=n_req, n_tensor=n_tensor),
        out_shape=(
            jax.ShapeDtypeStruct((rows, cols), BF16),
            jax.ShapeDtypeStruct((1, cols), BF16),
        ),
        in_specs=[pl.BlockSpec(memory_space=pltpu.HBM)] * len(args),
        out_specs=(
            pl.BlockSpec(memory_space=pltpu.VMEM),
            pl.BlockSpec(memory_space=pltpu.VMEM),
        ),
        scratch_shapes=scratch,
        compiler_params=pltpu.CompilerParams(
            collective_id=0, has_side_effects=True, vmem_limit_bytes=56 << 20
        ),
        name="layer",
    )(*args)


def solution(mesh):
    in_specs = (
        P("req", "tensor"),
        P("req", "tensor"),
        P(),
        P(),
        P(),
        P(),
        P("req", None, "tensor"),
        P("req", None, "tensor"),
        P(None, None, "tensor"),
        P("tensor", None),
        P(),
        P(),
        P(None, "tensor"),
        P("tensor", None),
        P(),
        P(),
    )
    out_specs = (P("req", "tensor"), P("req", "tensor"))
    body = functools.partial(local, n_req=mesh.shape["req"], n_tensor=mesh.shape["tensor"])
    return jax.shard_map(body, mesh=mesh, in_specs=in_specs, out_specs=out_specs, check_vma=False)
```
